32 devices in a mesh: row: 4 (over y, x), col: 8 (over z, core).
Axes of the slice: x: 2, y: 2, z: 4, core: 2. Of those that a mesh axis runs over, the one named last changes fastest.
Arguments:
- momentum: float32 [4096, 28672], P('row', 'col'), may hold values from -6 to 6
- gradient: bfloat16 [4096, 28672], P('row', 'col'), may hold values from -6 to 6
- weight: bfloat16 [4096, 28672], P('row', 'col'), may hold values from -3 to 3
- right_factor: float32 [28672, 512], P(('col', 'row')), may hold values from -0.03125 to 0.03125
Outputs:
- new_weight: bfloat16 [4096, 28672], P('row', 'col')
- new_momentum: float32 [4096, 28672], P('row', 'col')
- new_factor: float32 [28672, 512], P(('col', 'row'))
The draws below stay inside these ranges and needn't reach their ends.
All inputs are finite; a program needn't handle non-finite values.
Results may differ from the reference program's by a relative error of at most 0.0012.
Values sent between devices are 32-bit elements; how exact they have to be, the bound alone decides.
No kernel may reach another device: no remote copies, remote signals or barrier semaphores. Data moves between devices by JAX's collectives and lax.ppermute only.
A program may use at most 128 MiB of HBM per device.

```python
import jax
import jax.numpy as jnp
from jax import lax

ROWS = 4096
COLS = 28672
RANK = 512


def level_of(rng, extent, cuts, low, top_value):
    loudness, own = 1.0, jax.random.fold_in(rng, 6)
    for axis_at, blocks in cuts:
        heights = jnp.exp(jax.random.uniform(jax.random.fold_in(own, axis_at), (blocks,), jnp.float32, low / len(cuts), top_value / len(cuts)))
        loudness = loudness * jnp.repeat(heights, extent[axis_at] // blocks).reshape([-1 if axis == axis_at else 1 for axis in range(len(extent))])
    return loudness


def noise(own_key, extent, width, most, shards=(), dtype=jnp.bfloat16):
    array = width * jax.random.normal(own_key, extent, jnp.float32)
    if shards:
        array = array * level_of(own_key, extent, shards, -0.22, 0.18)
    return jnp.clip(array, -most, most).astype(dtype)


def setup_inputs(seed: int = 0) -> dict:
    seeds = jax.random.split(jax.random.key(seed), 5)
    return {
        "momentum": noise(seeds[0], (ROWS, COLS), 1.0, 6.0, ((0, 4), (1, 8)), jnp.float32),
        "gradient": noise(seeds[1], (ROWS, COLS), 1.0, 6.0, ((0, 4), (1, 8))),
        "weight": noise(seeds[2], (ROWS, COLS), 0.5, 3.0, ((0, 4), (1, 8))),
        "right_factor": noise(seeds[3], (COLS, RANK), COLS ** -0.5, 0.03125, ((0, 32),), jnp.float32),
    }


def reference(momentum, gradient, weight, right_factor):
    high = lax.Precision.HIGHEST
    buffer = momentum + gradient.astype(jnp.float32)
    proj = jnp.dot(buffer.astype(jnp.float32), right_factor.astype(jnp.float32), precision=high, preferred_element_type=jnp.float32)
    gram = jnp.dot(proj.T.astype(jnp.float32), proj.astype(jnp.float32), precision=high, preferred_element_type=jnp.float32)
    chol = jnp.linalg.cholesky(gram)
    ortho = lax.linalg.triangular_solve(chol, proj, left_side=False, lower=True, transpose_a=True)
    right = jnp.dot(buffer.T.astype(jnp.float32), ortho.astype(jnp.float32), precision=high, preferred_element_type=jnp.float32)
    scale = lax.rsqrt(lax.optimization_barrier(jnp.sum(right * right, axis=0)) + 1e-06)
    new_factor = right * scale
    new_momentum = buffer - 0.05 * jnp.dot(ortho.astype(jnp.float32), right.T.astype(jnp.float32), precision=high, preferred_element_type=jnp.float32)
    coef = 0.3 * (ROWS * COLS / RANK) ** 0.5
    update = jnp.dot(ortho.astype(jnp.float32), new_factor.T.astype(jnp.float32), precision=high, preferred_element_type=jnp.float32)
    new_weight = (weight.astype(jnp.float32) - coef * update).astype(jnp.bfloat16)
    return (new_weight, new_momentum, new_factor)
```

```python
import functools

import jax
import jax.numpy as jnp
from jax import lax
from jax.experimental import pallas as pl
from jax.experimental.pallas import tpu as pltpu
from jax.sharding import PartitionSpec as P

ROWS = 4096
COLS = 28672
RANK = 512
F32 = jnp.float32
BF16 = jnp.bfloat16
HIGHEST = lax.Precision.HIGHEST
CHUNKS = 2
NB = 128
VMEM = pl.BlockSpec(memory_space=pltpu.VMEM)
LIMIT = 56 * 2**20


def general(momentum, gradient, weight, right_factor):
    high = HIGHEST
    buffer = momentum + gradient.astype(F32)
    whole = lax.all_gather(right_factor, "row", axis=0, tiled=True)
    partial_proj = jnp.dot(buffer, whole, precision=high, preferred_element_type=F32)
    proj = lax.psum(partial_proj, "col")
    gram = lax.psum(jnp.dot(proj.T, proj, precision=high, preferred_element_type=F32), "row")
    chol = jnp.linalg.cholesky(gram)
    ortho = lax.linalg.triangular_solve(chol, proj, left_side=False, lower=True, transpose_a=True)
    share = lax.dot_general(
        buffer, ortho, (((0,), (0,)), ((), ())), precision=high, preferred_element_type=F32
    )
    right_share = lax.psum_scatter(share, "row", scatter_dimension=0, tiled=True)
    squares = lax.psum(jnp.sum(right_share * right_share, axis=0), ("row", "col"))
    scale = lax.rsqrt(squares + 1e-06)
    new_factor = right_share * scale
    right = lax.all_gather(right_share, "row", axis=0, tiled=True)
    new_momentum = buffer - 0.05 * jnp.dot(
        ortho, right.T, precision=high, preferred_element_type=F32
    )
    coef = 0.3 * (ROWS * COLS / RANK) ** 0.5
    update = jnp.dot(ortho, (right * scale).T, precision=high, preferred_element_type=F32)
    new_weight = (weight.astype(F32) - coef * update).astype(BF16)
    return (new_weight, new_momentum, new_factor)


def split(x):
    hi = x.astype(BF16)
    return hi, (x - hi.astype(F32)).astype(BF16)


def mul(a, b, ca=1, cb=0):
    return lax.dot_general(a, b, (((ca,), (cb,)), ((), ())), preferred_element_type=F32)


def exact(a, b, ca=1, cb=0):
    return lax.dot_general(
        a, b, (((ca,), (cb,)), ((), ())), precision=HIGHEST, preferred_element_type=F32
    )


def params(**kw):
    return pltpu.CompilerParams(vmem_limit_bytes=LIMIT, **kw)


def cost(flops, nbytes):
    return pl.CostEstimate(flops=int(flops), bytes_accessed=int(nbytes), transcendentals=0)


def proj_kernel(n, first, col_ref, row_ref, *refs):
    m_ref, g_ref = refs[:2]
    pieces = refs[2 : 2 + n]
    accs = refs[2 + n : -4] if not first else ()
    outs = refs[-4:-2]
    rh, rl = refs[-2:]
    k, i = pl.program_id(0), pl.program_id(1)
    tm = m_ref.shape[0]

    @pl.when(i == 0)
    def _():
        for p in range(n):

            @pl.when(k == p)
            def _(p=p):
                rh[...], rl[...] = split(pieces[p][...])

    ah, al = split(m_ref[...] + g_ref[...].astype(F32))
    term = mul(ah, rh[...]) + mul(ah, rl[...]) + mul(al, rh[...])
    half = pl.num_programs(1) // 2
    for s in range(2):

        @pl.when(i // half == s)
        def _(s=s):
            at = pl.ds(pl.multiple_of((i % half) * tm, tm), tm)

            @pl.when(k == 0)
            def _():
                outs[s][at, :] = term if first else accs[s][at, :] + term

            @pl.when(k != 0)
            def _():
                outs[s][at, :] += term


def proj_call(momentum, gradient, pieces, cols, rows, acc, name):
    n, nt = len(pieces), rows.shape[0]
    tm = momentum.shape[0] // nt
    kp, c = pieces[0].shape
    first = acc is None
    accs = () if first else tuple(acc)
    half = momentum.shape[0] // 2
    spec = pl.BlockSpec((tm, kp), lambda k, i, col, row: (row[i], col[k]))
    full = lambda shape: pl.BlockSpec(shape, lambda k, i, col, row: (0, 0))
    out = jax.ShapeDtypeStruct((half, c), F32)
    return pl.pallas_call(
        functools.partial(proj_kernel, n, first),
        grid_spec=pltpu.PrefetchScalarGridSpec(
            num_scalar_prefetch=2,
            grid=(n, nt),
            in_specs=[spec, spec] + [full((kp, c))] * n + [full((half, c))] * len(accs),
            out_specs=[full((half, c))] * 2,
            scratch_shapes=[pltpu.VMEM((kp, c), BF16)] * 2,
        ),
        out_shape=[out, out],
        compiler_params=params(),
        name=name,
        cost_estimate=cost(6 * n * kp * c * momentum.shape[0], 6 * n * kp * momentum.shape[0]),
    )(cols, rows, momentum, gradient, *pieces, *accs)


def right_kernel(nt, add, col_ref, row_ref, m_ref, g_ref, *refs):
    pieces, outs = refs[:nt], refs[-2:]
    i = pl.program_id(0)
    bh, bl = split(m_ref[...] + g_ref[...].astype(F32))
    h = outs[0].shape[0]
    for p in range(nt):

        @pl.when(i == p)
        def _(p=p):
            ph, pl_ = split(pieces[p][...].T)
            term = mul(ph, bh) + mul(ph, bl) + mul(pl_, bh)
            for s in range(2):
                part = term[s * h : (s + 1) * h, :]
                if p == 0:
                    outs[s][...] = part + refs[nt][...] if s == add else part
                else:
                    outs[s][...] += part


def right_call(momentum, gradient, pieces, col, rows, got, add, name):
    nt = rows.shape[0]
    tm, c = pieces[0].shape
    kp = momentum.shape[1] // 4
    extra = () if got is None else (got,)
    spec = pl.BlockSpec((tm, kp), lambda i, col, row: (row[i], col[0]))
    full = lambda shape: pl.BlockSpec(shape, lambda i, col, row: (0, 0))
    out = jax.ShapeDtypeStruct((c // 2, kp), F32)
    return pl.pallas_call(
        functools.partial(right_kernel, nt, add),
        grid_spec=pltpu.PrefetchScalarGridSpec(
            num_scalar_prefetch=2,
            grid=(nt,),
            in_specs=[spec, spec] + [full((tm, c))] * nt + [full((c // 2, kp))] * len(extra),
            out_specs=[full((c // 2, kp))] * 2,
        ),
        out_shape=[out, out],
        compiler_params=params(),
        name=name,
        cost_estimate=cost(6 * kp * c * momentum.shape[0], 6 * kp * momentum.shape[0]),
    )(col, rows, momentum, gradient, *pieces, *extra)


def gram_kernel(nt, core_ref, *refs):
    ins, outs = refs[:-2], refs[-2:]
    nc = len(ins) // nt
    c = ins[0].shape[1]
    per = nc // 2
    for s in range(2):

        @pl.when(core_ref[0] == s)
        def _(s=s):
            for j in range(nc):
                for q in range(per):
                    total = None
                    for p in range(nt):
                        term = exact(ins[(s * per + q) * nt + p][...], ins[j * nt + p][...], 0, 0)
                        total = term if total is None else total + term
                    h = outs[0].shape[0]
                    for o in range(2):
                        lo = o * h - q * c
                        if 0 <= lo < c:
                            outs[o][:, j * c : (j + 1) * c] = total[lo : lo + h, :]


def gram_call(chunks, core):
    nt, nc = len(chunks[0]), len(chunks)
    c = chunks[0][0].shape[1]
    rank = nc * c
    out = jax.ShapeDtypeStruct((rank // 4, rank), F32)
    return pl.pallas_call(
        functools.partial(gram_kernel, nt),
        grid_spec=pltpu.PrefetchScalarGridSpec(
            num_scalar_prefetch=1,
            grid=(),
            in_specs=[VMEM] * (nt * nc),
            out_specs=[VMEM] * 2,
        ),
        out_shape=[out, out],
        compiler_params=params(),
        name="gram",
        cost_estimate=cost(6 * rank * rank * 1024, 4 * 2**20),
    )(core, *[x for chunk in chunks for x in chunk])


def eliminate(d):
    n = d.shape[0]
    gs = n // 8
    sub = lax.broadcasted_iota(jnp.int32, (8, n), 0)
    lane = lax.broadcasted_iota(jnp.int32, (8, n), 1)
    left = [d[8 * g : 8 * g + 8, :] for g in range(gs)]
    right = [jnp.where(lane == sub + 8 * g, 1.0, 0.0).astype(F32) for g in range(gs)]
    for g in range(gs):
        for jj in range(8):
            j = 8 * g + jj
            col = [jnp.broadcast_to(left[t][:, j : j + 1], (8, n)) for t in range(g, gs)]
            inv = 1.0 / col[0][jj : jj + 1, :]
            row_l = jnp.broadcast_to(left[g][jj : jj + 1, :] * inv, (8, n))
            row_r = jnp.broadcast_to(right[g][jj : jj + 1, :] * inv, (8, n))
            for t in range(g, gs):
                c = col[t - g]
                if t == g:
                    if jj == 7:
                        continue
                    c = jnp.where(sub > jj, c, 0.0)
                left[t] = left[t] - c * row_l
                right[t] = right[t] - c * row_r
    out = []
    for g in range(gs):
        pivot = jnp.sum(jnp.where(lane == sub + 8 * g, left[g], 0.0), axis=1, keepdims=True)
        out.append(right[g] * lax.rsqrt(pivot))
    return jnp.concatenate(out, axis=0)


def chol_kernel(core_ref, mine_ref, other_ref, o_ref, a_ref):
    n = o_ref.shape[0]
    h = n // 2
    for s in range(2):

        @pl.when(core_ref[0] == s)
        def _(s=s):
            a_ref[s * h : (s + 1) * h, :] = mine_ref[...]
            a_ref[(1 - s) * h : (2 - s) * h, :] = other_ref[...]

    r = lax.broadcasted_iota(jnp.int32, (n, n), 0)
    c = lax.broadcasted_iota(jnp.int32, (n, n), 1)
    o_ref[...] = jnp.where(r == c, 1.0, 0.0).astype(F32)

    def body(k, carry):
        k0 = pl.multiple_of(k * NB, NB)
        x = eliminate(a_ref[pl.ds(k0, NB), pl.ds(k0, NB)])
        rows = lax.broadcasted_iota(jnp.int32, (n, NB), 0)
        panel = jnp.where(rows >= k0 + NB, exact(a_ref[:, pl.ds(k0, NB)], x, 1, 1), 0.0)
        band = exact(x, o_ref[pl.ds(k0, NB), :])
        o_ref[pl.ds(k0, NB), :] = band
        a_ref[...] = a_ref[...] - exact(panel, panel, 1, 1)
        o_ref[...] = o_ref[...] - exact(panel, band)
        return carry

    lax.fori_loop(0, n // NB, body, 0)


def chol_call(mine, other, core):
    n = mine.shape[1]
    return pl.pallas_call(
        chol_kernel,
        grid_spec=pltpu.PrefetchScalarGridSpec(
            num_scalar_prefetch=1,
            grid=(),
            in_specs=[VMEM] * 2,
            out_specs=VMEM,
            scratch_shapes=[pltpu.VMEM((n, n), F32)],
        ),
        out_shape=jax.ShapeDtypeStruct((n, n), F32),
        compiler_params=params(),
        name="cholinv",
        cost_estimate=cost(5 * 10**10, 2 * 2**20),
    )(core, mine, other)


def ortho_kernel(nt, nc, row_ref, inv_ref, *refs):
    o_ref = refs[-1]
    i = pl.program_id(0)
    for p in range(nt):

        @pl.when(i == p)
        def _(p=p):
            x = jnp.concatenate([refs[j * nt + p][...] for j in range(nc)], axis=1)
            o_ref[...] = exact(x, inv_ref[...], 1, 1)


def ortho_call(chunks, inv, rows):
    nt, nc = len(chunks[0]), len(chunks)
    tm, c = chunks[0][0].shape
    full = lambda shape: pl.BlockSpec(shape, lambda i, row: (0, 0))
    return pl.pallas_call(
        functools.partial(ortho_kernel, nt, nc),
        grid_spec=pltpu.PrefetchScalarGridSpec(
            num_scalar_prefetch=1,
            grid=(nt,),
            in_specs=[full(inv.shape)] + [full((tm, c))] * (nt * nc),
            out_specs=pl.BlockSpec((tm, nc * c), lambda i, row: (row[i], 0)),
        ),
        out_shape=jax.ShapeDtypeStruct((nt * tm, nc * c), F32),
        compiler_params=params(),
        name="ortho",
        cost_estimate=cost(6 * nt * tm * (nc * c) ** 2, 5 * 2**20),
    )(rows, inv, *[x for chunk in chunks for x in chunk])


def share_kernel(inv_ref, *refs):
    o_ref, s_ref = refs[-2:]
    x = jnp.concatenate([r[...] for r in refs[:-2]], axis=0)
    r = exact(x, inv_ref[...], 0, 1)
    o_ref[...] = r
    s_ref[...] = jnp.sum(r * r, axis=0, keepdims=True)


def share_call(shares, inv):
    kp = shares[0].shape[1]
    n = inv.shape[0]
    return pl.pallas_call(
        share_kernel,
        in_specs=[VMEM] * (1 + len(shares)),
        out_specs=[VMEM] * 2,
        out_shape=[jax.ShapeDtypeStruct((kp, n), F32), jax.ShapeDtypeStruct((1, n), F32)],
        compiler_params=params(),
        name="share",
        cost_estimate=cost(6 * kp * n * n, 5 * 2**20),
    )(inv, *shares)


def update_kernel(groups, coef, col_ref, scale_ref, inv_ref, ortho_ref, m_ref, g_ref, w_ref, *refs):
    total = sum(len(x) for x in groups)
    pieces = refs[:total]
    w_out, m_out, oh, sh, sl, ih, il, rh, rl = refs[-9:]
    k, i = pl.program_id(0), pl.program_id(1)
    tm = m_ref.shape[0]

    @pl.when((k == 0) & (i == 0))
    def _():
        o = ortho_ref[...]
        oh[...] = (0.05 * o).astype(BF16)
        sh[...], sl[...] = split(o * (coef * scale_ref[...]))
        ih[...], il[...] = split(inv_ref[...])

    @pl.when(i == 0)
    def _():
        at = 0
        for q, group in enumerate(groups):
            mine = pieces[at : at + len(group)]
            at += len(group)

            @pl.when(k == q)
            def _(mine=mine):
                x = jnp.concatenate([r[...] for r in mine], axis=0)
                xh, xl = split(x)
                r = mul(ih[...], xh) + mul(ih[...], xl) + mul(il[...], xh)
                rh[...], rl[...] = split(r)

    rows = pl.ds(pl.multiple_of(i * tm, tm), tm)
    m_out[...] = m_ref[...] + g_ref[...].astype(F32) - mul(oh[rows, :], rh[...])
    up = mul(sh[rows, :], rh[...]) + mul(sh[rows, :], rl[...]) + mul(sl[rows, :], rh[...])
    w_out[...] = (w_ref[...].astype(F32) - up).astype(BF16)


def update_call(momentum, gradient, weight, ortho, inv, scale, groups, cols, coef, before, name):
    n = len(groups)
    rows, width = momentum.shape
    kp = width // 4
    tm = rows // 2
    rank = inv.shape[0]
    pieces = [x for group in groups for x in group]
    spec = pl.BlockSpec((tm, kp), lambda k, i, col: (i, col[k]))
    full = lambda shape: pl.BlockSpec(shape, lambda k, i, col: (0, 0))
    extra = () if before is None else tuple(before)
    aliases = {} if before is None else {7 + len(pieces): 0, 8 + len(pieces): 1}
    return pl.pallas_call(
        functools.partial(update_kernel, [[0] * len(g) for g in groups], coef),
        grid_spec=pltpu.PrefetchScalarGridSpec(
            num_scalar_prefetch=1,
            grid=(n, 2),
            in_specs=[full((1, rank)), full((rank, rank)), full((rows, rank)), spec, spec, spec]
            + [full(x.shape) for x in pieces]
            + [pl.BlockSpec(memory_space=pl.ANY)] * len(extra),
            out_specs=[spec, spec],
            scratch_shapes=[pltpu.VMEM((rows, rank), BF16)] * 3
            + [pltpu.VMEM((rank, rank), BF16)] * 2
            + [pltpu.VMEM((rank, kp), BF16)] * 2,
        ),
        out_shape=[
            jax.ShapeDtypeStruct((rows, width), BF16),
            jax.ShapeDtypeStruct((rows, width), F32),
        ],
        input_output_aliases=aliases,
        compiler_params=params(),
        name=name,
        cost_estimate=cost(11 * n * kp * rows * rank, 14 * n * kp * rows),
    )(cols, scale, inv, ortho, momentum, gradient, weight, *pieces, *extra)


def along(axis, size, flip):
    return lambda a: lax.ppermute(a, axis, [(s, s ^ flip) for s in range(size)])


def pick(x, parts, which):
    size = x.shape[0] // parts
    return lax.dynamic_slice_in_dim(x, which * size, size, 0)


def square(momentum, gradient, weight, right_factor):
    row, col = lax.axis_index("row"), lax.axis_index("col")
    to_x, to_y, to_d = (along("row", 4, f) for f in (1, 2, 3))
    to_core, to_z, to_zz, to_zzz = (along("col", 8, f) for f in (1, 2, 4, 6))
    core, z0 = col % 2, (col // 2) % 2
    tile = jnp.arange(4, dtype=jnp.int32) ^ (core * 2 + z0)
    piece = jnp.arange(4, dtype=jnp.int32) ^ row
    core1 = jnp.reshape(core, (1,)).astype(jnp.int32)
    c = right_factor.shape[1] // CHUNKS

    def gather(own):
        h = own.shape[0] // 2
        bx, by = to_x(own), to_y(own)
        return own, bx, by, to_x(by[:h]), to_y(bx[h:])

    projs = []
    for q in range(CHUNKS):
        own, bx, by, d0, d1 = gather(right_factor[:, q * c : (q + 1) * c])
        acc = proj_call(momentum, gradient, [own], piece[:1], tile, None, f"proj_own{q}")
        acc = proj_call(momentum, gradient, [bx, by], piece[1:3], tile, acc, f"proj_xy{q}")
        diag = jnp.concatenate([d0, d1], axis=0)
        keep, give = proj_call(momentum, gradient, [diag], piece[3:], tile, acc, f"proj_d{q}")
        s = keep + to_core(give)
        h = s.shape[0] // 2
        t = s[:h] + to_z(s[h:])
        t = t + to_zz(t)
        o = to_z(t)
        projs.append((t, o, to_core(t), to_core(o)))

    ga, gb = gram_call(projs, core1)
    ga, gb = ga + to_x(ga), gb + to_y(gb)
    ga, gb = ga + to_y(ga), gb + to_x(gb)
    half = jnp.concatenate([ga, gb], axis=0)
    inv = chol_call(half, to_core(half), core1)

    shares, gathered = [], []
    for q in range(CHUNKS):
        call = lambda s, got, add, name: right_call(
            momentum, gradient, projs[q], piece[s : s + 1], tile, got, add, f"right_{name}{q}"
        )
        da, db = call(3, None, -1, "d")
        oa, ob = call(0, None, -1, "o")
        got_x, got_y = to_x(da), to_y(db)
        ya, yb = call(2, got_x, 0, "y")
        xa, xb = call(1, got_y, 1, "x")
        fxa, fxb, fya, fyb = to_x(xa), to_x(xb), to_y(ya), to_y(yb)
        own = jnp.concatenate([oa + fxa + fya, ob + fxb + fyb], axis=0)
        shares.append(own)
        gathered.append(gather(own))

    right_share, squares = share_call(shares, inv)
    squares = squares + to_x(squares) + to_y(squares) + to_d(squares)
    squares = squares + to_core(squares)
    squares = squares + to_z(squares) + to_zz(squares) + to_zzz(squares)
    scale = lax.rsqrt(squares + 1e-06)
    new_factor = right_share * scale
    ortho = ortho_call(projs, inv, tile)
    coef = 0.3 * (ROWS * COLS / RANK) ** 0.5
    args = (momentum, gradient, weight, ortho, inv, scale)
    owns, xs, ys = ([g[s] for g in gathered] for s in range(3))
    ds = [x for g in gathered for x in g[3:]]
    out = update_call(*args, [owns], piece[:1], coef, None, "update_own")
    out = update_call(*args, [xs, ys], piece[1:3], coef, out, "update_xy")
    new_weight, new_momentum = update_call(*args, [ds], piece[3:], coef, out, "update_d")
    return (new_weight, new_momentum, new_factor)


def solution(mesh):
    rows, cols = mesh.shape["row"], mesh.shape["col"]

    def per_device(momentum, gradient, weight, right_factor):
        fits = (
            rows == 4
            and cols == 8
            and momentum.shape[0] % 1024 == 0
            and momentum.shape[1] % 512 == 0
            and right_factor.shape[1] == 512
        )
        body = square if fits else general
        return body(momentum, gradient, weight, right_factor)

    return jax.shard_map(
        per_device,
        mesh=mesh,
        in_specs=(P("row", "col"), P("row", "col"), P("row", "col"), P(("col", "row"), None)),
        out_specs=(P("row", "col"), P("row", "col"), P(("col", "row"), None)),
        check_vma=False,
    )
```

```python
import functools

import jax
import jax.numpy as jnp
from jax import lax
from jax.experimental import pallas as pl
from jax.experimental.pallas import tpu as pltpu
from jax.sharding import PartitionSpec as P


ROWS = 4096
COLS = 28672
RANK = 512
F32 = jnp.float32
BF16 = jnp.bfloat16
HIGHEST = lax.Precision.HIGHEST
NB = 128
HALF = 256
VMEM = pl.BlockSpec(memory_space=pltpu.VMEM)
LIMIT = 40 * 2**20
WIDE = 56 * 2**20


def general(momentum, gradient, weight, right_factor):
    high = HIGHEST
    buffer = momentum + gradient.astype(F32)
    whole = lax.all_gather(right_factor, "row", axis=0, tiled=True)
    partial_proj = jnp.dot(buffer, whole, precision=high, preferred_element_type=F32)
    proj = lax.psum(partial_proj, "col")
    gram = lax.psum(jnp.dot(proj.T, proj, precision=high, preferred_element_type=F32), "row")
    chol = jnp.linalg.cholesky(gram)
    ortho = lax.linalg.triangular_solve(chol, proj, left_side=False, lower=True, transpose_a=True)
    share = lax.dot_general(
        buffer, ortho, (((0,), (0,)), ((), ())), precision=high, preferred_element_type=F32
    )
    right_share = lax.psum_scatter(share, "row", scatter_dimension=0, tiled=True)
    squares = lax.psum(jnp.sum(right_share * right_share, axis=0), ("row", "col"))
    scale = lax.rsqrt(squares + 1e-06)
    new_factor = right_share * scale
    right = lax.all_gather(right_share, "row", axis=0, tiled=True)
    new_momentum = buffer - 0.05 * jnp.dot(
        ortho, right.T, precision=high, preferred_element_type=F32
    )
    coef = 0.3 * (ROWS * COLS / RANK) ** 0.5
    update = jnp.dot(ortho, (right * scale).T, precision=high, preferred_element_type=F32)
    new_weight = (weight.astype(F32) - coef * update).astype(BF16)
    return (new_weight, new_momentum, new_factor)


def split(x):
    hi = x.astype(BF16)
    return hi, (x - hi.astype(F32)).astype(BF16)


def mul(a, b, ca=1, cb=0):
    return lax.dot_general(a, b, (((ca,), (cb,)), ((), ())), preferred_element_type=F32)


def exact(a, b, ca=1, cb=0):
    return lax.dot_general(
        a, b, (((ca,), (cb,)), ((), ())), precision=HIGHEST, preferred_element_type=F32
    )


def params(limit=LIMIT):
    return pltpu.CompilerParams(vmem_limit_bytes=limit)


def cost(flops, nbytes):
    return pl.CostEstimate(flops=int(flops), bytes_accessed=int(nbytes), transcendentals=0)


def mul3(a, b, ca=1, cb=0):
    (ah, al), (bh, bl) = a, b
    return mul(ah, bh, ca, cb) + mul(ah, bl, ca, cb) + mul(al, bh, ca, cb)


def whole_spec(shape):
    return pl.BlockSpec(shape, lambda *_: (0,) * len(shape))


def split_kernel(m_ref, g_ref, h_ref, l_ref):
    h_ref[...], l_ref[...] = split(m_ref[...] + g_ref[...].astype(F32))


def split_call(momentum, gradient):
    rows, width = momentum.shape
    spec = pl.BlockSpec((rows // 8, width), lambda i: (i, 0))
    out = jax.ShapeDtypeStruct(momentum.shape, BF16)
    return pl.pallas_call(
        split_kernel,
        grid=(8,),
        in_specs=[spec] * 2,
        out_specs=[spec] * 2,
        out_shape=[out] * 2,
        compiler_params=params(),
        name="split",
        cost_estimate=cost(4 * rows * width, 10 * rows * width),
    )(momentum, gradient)


def proj_kernel(sizes, first, col_ref, row_ref, z_ref, bh_ref, bl_ref, *refs):
    groups, accs = refs[: sum(sizes)], refs[sum(sizes) : -4]
    outs = refs[-4:-2]
    rh, rl = refs[-2:]
    k, i = pl.program_id(0), pl.program_id(1)

    @pl.when(i == 0)
    def _():
        for p, size in enumerate(sizes):
            mine = groups[sum(sizes[:p]) : sum(sizes[: p + 1])]

            @pl.when(k == p)
            def _(mine=mine):
                h = mine[0].shape[0]
                for q, ref in enumerate(mine):
                    at = slice(q * h, (q + 1) * h)
                    rh[at, :], rl[at, :] = split(ref[...])

    term = mul3((bh_ref[...], bl_ref[...]), (rh[...], rl[...]))
    h = term.shape[0] // 2
    for s in range(2):

        @pl.when(i == s)
        def _(s=s):
            for u in range(2):
                at = pl.ds(pl.multiple_of((u ^ z_ref[0]) * h, h), h)
                part = term[u * h : (u + 1) * h, :]

                @pl.when(k == 0)
                def _():
                    outs[s][at, :] = part if first else accs[s][at, :] + part

                @pl.when(k != 0)
                def _():
                    outs[s][at, :] += part


def proj_call(pair, groups, cols, rows, z0, acc):
    n = len(groups)
    pieces = [x for group in groups for x in group]
    tm = pair[0].shape[0] // 2
    kp, c = pair[0].shape[1] // 4, pieces[0].shape[1]
    accs = () if acc is None else tuple(acc)
    spec = pl.BlockSpec((tm, kp), lambda k, i, col, row, z: (row[i], col[k]))
    out = jax.ShapeDtypeStruct((tm, c), F32)
    return pl.pallas_call(
        functools.partial(proj_kernel, [len(g) for g in groups], acc is None),
        grid_spec=pltpu.PrefetchScalarGridSpec(
            num_scalar_prefetch=3,
            grid=(n, 2),
            in_specs=[spec] * 2 + [whole_spec(x.shape) for x in pieces] + [whole_spec((tm, c))] * len(accs),
            out_specs=[whole_spec((tm, c))] * 2,
            scratch_shapes=[pltpu.VMEM((kp, c), BF16)] * 2,
        ),
        out_shape=[out] * 2,
        compiler_params=params(),
        cost_estimate=cost(12 * n * kp * c * tm, 8 * n * kp * tm),
    )(cols, rows, z0, *pair, *pieces, *accs)


def prep_kernel(nt, row_ref, core_ref, *refs):
    h_ref, l_ref, g_ref = refs[-3:]
    own, others = refs[:nt], refs[nt:-3]
    tm = own[0].shape[0]
    turned = []
    for p in range(nt):
        x = own[p][...].T
        at = pl.ds(pl.multiple_of(row_ref[p] * tm, tm), tm)
        h_ref[:, at], l_ref[:, at] = split(x)
        turned.append(x)

    def gram(with_):
        total = exact(turned[0], with_[0][...])
        for p in range(1, nt):
            total = total + exact(turned[p], with_[p][...])
        g_ref[...] = total

    if others:
        pl.when(core_ref[0] == 0)(lambda: gram(others))
        pl.when(core_ref[0] == 1)(lambda: gram(own))
    else:
        gram(own)


def prep_call(own, others, rows, core):
    nt = len(own)
    tm, c = own[0].shape
    turned = jax.ShapeDtypeStruct((c, nt * tm), BF16)
    return pl.pallas_call(
        functools.partial(prep_kernel, nt),
        grid_spec=pltpu.PrefetchScalarGridSpec(
            num_scalar_prefetch=2,
            grid=(),
            in_specs=[VMEM] * (nt + len(others)),
            out_specs=[VMEM] * 3,
        ),
        out_shape=[turned, turned, jax.ShapeDtypeStruct((c, c), F32)],
        compiler_params=params(),
        cost_estimate=cost(12 * nt * tm * c * c, 3 * 2**20),
    )(rows, core, *own, *others)


def far_kernel(col_ref, ph_ref, pl_ref, bh_ref, bl_ref, a_ref, b_ref, o_ref):
    k = pl.program_id(0)
    term = mul3((ph_ref[...], pl_ref[...]), (bh_ref[...], bl_ref[...]))
    h = a_ref.shape[0]

    @pl.when(k == 0)
    def _():
        a_ref[...], b_ref[...] = term[:h, :], term[h:, :]

    @pl.when(k == 1)
    def _():
        o_ref[...] = term


def halves_kernel(col_ref, ph_ref, pl_ref, bh_ref, bl_ref, *refs):
    k = pl.program_id(0)
    term = mul3((ph_ref[...], pl_ref[...]), (bh_ref[...], bl_ref[...]))
    h = refs[0].shape[0]
    for s in range(2):

        @pl.when(k == s)
        def _(s=s):
            refs[2 * s][...], refs[2 * s + 1][...] = term[:h, :], term[h:, :]


def right_call(kernel, pair, turned, cols):
    rows, width = pair[0].shape
    c = turned[0].shape[0]
    kp = width // 4
    spec = pl.BlockSpec((rows, kp), lambda k, col: (0, col[k]))
    full, half = ((c, kp), (c // 2, kp))
    outs = [half] * 2 + [full] if kernel is far_kernel else [half] * 4
    return pl.pallas_call(
        kernel,
        grid_spec=pltpu.PrefetchScalarGridSpec(
            num_scalar_prefetch=1,
            grid=(2,),
            in_specs=[whole_spec((c, rows))] * 2 + [spec] * 2,
            out_specs=[whole_spec(s) for s in outs],
        ),
        out_shape=[jax.ShapeDtypeStruct(s, F32) for s in outs],
        compiler_params=params(),
        cost_estimate=cost(12 * kp * c * rows, 8 * kp * rows),
    )(cols, *turned, *pair)


def eliminate(d):
    n = d.shape[0]
    gs = n // 8
    sub = lax.broadcasted_iota(jnp.int32, (8, n), 0)
    lane = lax.broadcasted_iota(jnp.int32, (8, n), 1)
    left = [d[8 * g : 8 * g + 8, :] for g in range(gs)]
    right = [jnp.where(lane == sub + 8 * g, 1.0, 0.0).astype(F32) for g in range(gs)]
    wide = lambda x: jnp.broadcast_to(x, (8, n))
    for g in range(gs):
        cols = [
            [wide(left[t][:, 8 * g + e : 8 * g + e + 1]) for e in range(8)] for t in range(g, gs)
        ]
        for e in range(8):
            inv = 1.0 / wide(cols[0][e][e : e + 1, :])
            row_l = wide(left[g][e : e + 1, :]) * inv
            row_r = wide(right[g][e : e + 1, :]) * inv
            ahead = [wide(cols[0][f][e : e + 1, :]) * inv for f in range(e + 1, 8)]
            for t in range(g, gs):
                c = cols[t - g][e]
                if t == g:
                    if e == 7:
                        continue
                    c = jnp.where(sub > e, c, 0.0)
                for f in range(e + 1, 8):
                    cols[t - g][f] = cols[t - g][f] - c * ahead[f - e - 1]
                left[t] = left[t] - c * row_l
                right[t] = right[t] - c * row_r
    out = []
    for g in range(gs):
        pivot = jnp.sum(jnp.where(lane == sub + 8 * g, left[g], 0.0), axis=1, keepdims=True)
        out.append(right[g] * lax.rsqrt(pivot))
    return jnp.concatenate(out, axis=0)


def chol_inverse(a_ref, o_ref):
    def body(k, carry):
        at = pl.ds(pl.multiple_of(k * NB, NB), NB)
        o_ref[at, at] = eliminate(a_ref[at, at])

        @pl.when(k == 0)
        def _():
            panel = exact(a_ref[NB:, :NB], o_ref[:NB, :NB], 1, 1)
            a_ref[NB:, NB:] = a_ref[NB:, NB:] - exact(panel, panel, 1, 1)
            a_ref[NB:, :NB] = panel

        return carry

    lax.fori_loop(0, 2, body, 0)
    o_ref[:NB, NB:] = jnp.zeros((NB, NB), F32)
    o_ref[NB:, :NB] = -exact(o_ref[NB:, NB:], exact(a_ref[NB:, :NB], o_ref[:NB, :NB]))


def chol_first(g_ref, o_ref, a_ref):
    a_ref[...] = g_ref[...]
    chol_inverse(a_ref, o_ref)


def chol_second(core_ref, mine_ref, other_ref, x_ref, h_ref, l_ref, a_ref, o_ref):
    n = x_ref.shape[0]
    first = core_ref[0] == 0
    below = jnp.where(first, mine_ref[...], other_ref[...])
    corner = jnp.where(first, other_ref[...], mine_ref[...])
    x = x_ref[...]
    panel = exact(below, x, 1, 1)
    a_ref[...] = corner - exact(panel, panel, 1, 1)
    chol_inverse(a_ref, o_ref)
    y = o_ref[...]
    h_ref[:n, n:] = jnp.zeros((n, n), BF16)
    l_ref[:n, n:] = jnp.zeros((n, n), BF16)
    h_ref[:n, :n], l_ref[:n, :n] = split(x)
    h_ref[n:, n:], l_ref[n:, n:] = split(y)
    h_ref[n:, :n], l_ref[n:, :n] = split(-exact(y, exact(panel, x)))


def chol_calls(block, mine, other, core):
    n = block.shape[0]
    shape = jax.ShapeDtypeStruct((n, n), F32)
    x = pl.pallas_call(
        chol_first,
        in_specs=[VMEM],
        out_specs=VMEM,
        out_shape=shape,
        scratch_shapes=[pltpu.VMEM((n, n), F32)],
        compiler_params=params(),
        name="chol_first",
        cost_estimate=cost(10**10, 2**20),
    )(block)
    out = jax.ShapeDtypeStruct((2 * n, 2 * n), BF16)
    return pl.pallas_call(
        chol_second,
        grid_spec=pltpu.PrefetchScalarGridSpec(
            num_scalar_prefetch=1,
            grid=(),
            in_specs=[VMEM] * 3,
            out_specs=[VMEM] * 2,
            scratch_shapes=[pltpu.VMEM((n, n), F32)] * 2,
        ),
        out_shape=[out] * 2,
        compiler_params=params(),
        name="chol_second",
        cost_estimate=cost(10**10, 2**20),
    )(core, mine, other, x), x


def ortho_kernel(nt, nc, row_ref, ih_ref, il_ref, *refs):
    o_ref, h_ref = refs[-2:]
    i = pl.program_id(0)
    for p in range(nt):

        @pl.when(i == p)
        def _(p=p):
            x = jnp.concatenate([refs[j * nt + p][...] for j in range(nc)], axis=1)
            o = mul3(split(x), (ih_ref[...], il_ref[...]), 1, 1)
            o_ref[...] = o
            h_ref[...] = (0.05 * o).astype(BF16)


def ortho_call(chunks, inv, rows):
    nt, nc = len(chunks[0]), len(chunks)
    tm, c = chunks[0][0].shape
    spec = pl.BlockSpec((tm, nc * c), lambda i, row: (row[i], 0))
    return pl.pallas_call(
        functools.partial(ortho_kernel, nt, nc),
        grid_spec=pltpu.PrefetchScalarGridSpec(
            num_scalar_prefetch=1,
            grid=(nt,),
            in_specs=[whole_spec(inv[0].shape)] * 2 + [whole_spec((tm, c))] * (nt * nc),
            out_specs=[spec] * 2,
        ),
        out_shape=[
            jax.ShapeDtypeStruct((nt * tm, nc * c), F32),
            jax.ShapeDtypeStruct((nt * tm, nc * c), BF16),
        ],
        compiler_params=params(),
        name="ortho",
        cost_estimate=cost(6 * nt * tm * (nc * c) ** 2, 5 * 2**20),
    )(rows, *inv, *[x for chunk in chunks for x in chunk])


def turn_kernel(x_ref, a_ref, b_ref, o_ref):
    w = jnp.concatenate([a_ref[...], b_ref[...]], axis=0)
    o_ref[...] = mul3(split(x_ref[...]), split(w))


def turn_call(x, halves):
    shape = (x.shape[0], halves[0].shape[1])
    return pl.pallas_call(
        turn_kernel,
        in_specs=[VMEM] * 3,
        out_specs=VMEM,
        out_shape=jax.ShapeDtypeStruct(shape, F32),
        compiler_params=params(),
        name="turn",
        cost_estimate=cost(6 * shape[0] ** 2 * shape[1], 2 * 2**20),
    )(x, *halves)


def share_kernel(ih_ref, il_ref, t_ref, *refs):
    t_out, r_ref, s_ref = refs[-3:]
    c = t_ref.shape[0]
    w = jnp.concatenate([r[...] for r in refs[:-3]], axis=0)
    t_out[...] = mul3((ih_ref[c:, :], il_ref[c:, :]), split(w))
    r_ref[:, :c] = t_ref[...].T
    r_ref[:, c:] = t_out[...].T
    r = r_ref[...]
    s_ref[...] = jnp.sum(r * r, axis=0, keepdims=True)


def share_call(first, halves, inv):
    c, kp = first.shape
    n = inv[0].shape[0]
    shapes = (c, kp), (kp, n), (1, n)
    return pl.pallas_call(
        share_kernel,
        in_specs=[VMEM] * (3 + len(halves)),
        out_specs=[VMEM] * 3,
        out_shape=[jax.ShapeDtypeStruct(s, F32) for s in shapes],
        compiler_params=params(),
        name="share",
        cost_estimate=cost(6 * kp * n * c, 5 * 2**20),
    )(*inv, first, *halves)


def scale_kernel(coef, s_ref, r_ref, o_ref, f_ref, h_ref, l_ref):
    scale = lax.rsqrt(s_ref[...] + 1e-06)
    f_ref[...] = r_ref[...] * scale
    h_ref[...], l_ref[...] = split(o_ref[...] * (coef * scale))


def scale_call(squares, share, ortho, coef):
    rows, n = ortho.shape
    out = jax.ShapeDtypeStruct((rows, n), BF16)
    parts = 4
    spec = pl.BlockSpec((rows // parts, n), lambda i: (i, 0))
    fspec = pl.BlockSpec((share.shape[0] // parts, n), lambda i: (i, 0))
    return pl.pallas_call(
        functools.partial(scale_kernel, coef),
        grid=(parts,),
        in_specs=[whole_spec((1, n)), fspec, spec],
        out_specs=[fspec, spec, spec],
        out_shape=[jax.ShapeDtypeStruct(share.shape, F32), out, out],
        compiler_params=params(),
        name="scale",
        cost_estimate=cost(4 * rows * n, 12 * rows * n),
    )(squares, share, ortho)


def update_kernel(groups, with_m, with_w, col_ref, *refs):
    refs = list(refs)
    take = lambda count: [refs.pop(0) for _ in range(count)]
    oh, m_ref, g_ref = take(3) if with_m else (None,) * 3
    sh, sl, w_ref = take(3) if with_w else (None,) * 3
    pieces = take(sum(groups))
    rl, rh = refs.pop(), refs.pop()
    m_out = refs.pop() if with_m else None
    w_out = refs.pop() if with_w else None
    k, i = pl.program_id(0), pl.program_id(1)

    @pl.when(i == 0)
    def _():
        at = 0
        for q, size in enumerate(groups):
            mine = pieces[at : at + size]
            at += size

            @pl.when(k == q)
            def _(mine=mine):
                row = 0
                for ref in mine:
                    rows = slice(row, row + ref.shape[0])
                    rh[rows, :], rl[rows, :] = split(ref[...])
                    row += ref.shape[0]

    tm = (m_ref if with_m else w_ref).shape[0]
    rows = pl.ds(pl.multiple_of(i * tm, tm), tm)
    if with_m:
        m_out[...] = m_ref[...] + g_ref[...].astype(F32) - mul(oh[rows, :], rh[...])
    if with_w:
        up = mul3((sh[rows, :], sl[rows, :]), (rh[...], rl[...]))
        w_out[...] = (w_ref[...].astype(F32) - up).astype(BF16)


def update_call(for_m, for_w, groups, cols, before):
    n = len(groups)
    like = for_m[1] if for_m else for_w[2]
    rows, width = like.shape
    kp = width // 4
    tm = rows // 2
    pieces = [x for group in groups for x in group]
    rank = sum(x.shape[0] for x in groups[0])
    spec = pl.BlockSpec((tm, kp), lambda k, i, col: (i, col[k]))
    left = whole_spec((rows, rank))
    in_specs = ([left, spec, spec] if for_m else []) + ([left, left, spec] if for_w else [])
    in_specs += [whole_spec(x.shape) for x in pieces]
    outs = ([BF16] if for_w else []) + ([F32] if for_m else [])
    units = (1 if for_m else 0) + (3 if for_w else 0)
    return pl.pallas_call(
        functools.partial(update_kernel, [len(g) for g in groups], bool(for_m), bool(for_w)),
        grid_spec=pltpu.PrefetchScalarGridSpec(
            num_scalar_prefetch=1,
            grid=(n, 2),
            in_specs=in_specs + [pl.BlockSpec(memory_space=pl.ANY)] * len(before),
            out_specs=[spec] * len(outs),
            scratch_shapes=[pltpu.VMEM((rank, kp), BF16)] * 2,
        ),
        out_shape=[jax.ShapeDtypeStruct((rows, width), dtype) for dtype in outs],
        input_output_aliases={1 + len(in_specs) + e: e for e in range(len(before))},
        compiler_params=params(WIDE),
        cost_estimate=cost(2 * units * n * kp * rows * rank, 3 * units * n * kp * rows),
    )(cols, *for_m, *for_w, *pieces, *before)


def square(momentum, gradient, weight, right_factor):
    def move(a, axis, size, flip):
        return lax.ppermute(a, axis, [(s, s ^ flip) for s in range(size)])

    to_x = lambda a: move(a, "row", 4, 1)
    to_y = lambda a: move(a, "row", 4, 2)
    to_core = lambda a: move(a, "col", 8, 1)
    to_z = lambda a, flip=2: move(a, "col", 8, flip)
    row, col = lax.axis_index("row"), lax.axis_index("col")
    one = lambda x: jnp.reshape(x, (1,)).astype(jnp.int32)
    core, z0 = col % 2, (col // 2) % 2
    tile = jnp.arange(4, dtype=jnp.int32) ^ (core * 2 + z0)
    sides = jnp.arange(2, dtype=jnp.int32) ^ core
    piece = jnp.arange(4, dtype=jnp.int32) ^ row
    far, near = jnp.array([3, 0], jnp.int32) ^ row, piece[1:3]
    core, z0 = one(core), one(z0)
    coef = 0.3 * (ROWS * COLS / RANK) ** 0.5

    def first_hop(own):
        return to_x(own), to_y(own)

    def second_hop(bx, by):
        h = bx.shape[0] // 2
        return to_x(by[:h]), to_y(bx[h:])

    def add_cols(keep, give):
        s = keep + to_core(give)
        h = s.shape[0] // 2
        t = s[:h] + to_z(s[h:])
        t = t + to_z(t, 4)
        ct = to_core(t)
        o = to_z(t)
        return t, o, ct, to_core(o)

    def project(groups, cols, acc):
        return proj_call(pair, groups, cols, sides, z0, acc)

    own0, own1 = right_factor[:, :HALF], right_factor[:, HALF:]
    x0, y0 = first_hop(own0)
    pair = split_call(momentum, gradient)
    acc0 = project([[own0]], piece[:1], None)
    own1, x0, y0 = lax.optimization_barrier((own1, x0, y0))
    e0, f0 = second_hop(x0, y0)
    acc0 = project([[x0], [y0]], near, acc0)
    x1, y1 = first_hop(own1)
    proj0 = add_cols(*project([[e0, f0]], piece[3:], acc0))
    acc1 = project([[own1]], piece[:1], None)
    e1, f1 = second_hop(x1, y1)
    acc1 = project([[x1], [y1]], near, acc1)
    proj1 = add_cols(*project([[e1, f1]], piece[3:], acc1))

    def right(kernel, turned, cols):
        return right_call(kernel, pair, turned, cols)

    def sum_rows(turned):
        da, db, own = right(far_kernel, turned, far)
        got_x, got_y = to_x(da), to_y(db)
        xa, xb, ya, yb = right(halves_kernel, turned, near)
        xa, yb = to_x(xa), to_y(yb)
        xb, ya = to_x(xb + got_y), to_y(ya + got_x)
        h = xa.shape[0]
        return own[:h] + xa + ya, own[h:] + xb + yb

    def sum4(a):
        ax, ay = to_x(a), to_y(a)
        return (a + ax) + (ay + move(a, "row", 4, 3))

    *turned0, block = prep_call(proj0, (), tile, core)
    block = block + to_x(block)
    block = block + to_y(block)
    w0 = sum_rows(turned0)
    *turned1, mine = prep_call(proj1, proj0, tile, core)
    mine = sum4(mine)
    inv, corner = chol_calls(block, mine, to_core(mine), core)
    w1 = sum_rows(turned1)
    r0 = turn_call(corner, w0)
    a0, b0 = first_hop(r0)
    e0, f0 = second_hop(a0, b0)
    r1, share, squares = share_call(r0, [*w0, *w1], inv)
    squares = sum4(squares)
    squares = squares + to_core(squares)
    squares = (squares + to_z(squares)) + (to_z(squares, 4) + to_z(squares, 6))
    a1, b1 = first_hop(r1)
    e1, f1 = second_hop(a1, b1)
    ortho, left = ortho_call([proj0, proj1], inv, tile)
    new_factor, *lefts = scale_call(squares, share, ortho, coef)
    for_m, for_w = (left, momentum, gradient), (*lefts, weight)

    def update(for_m, for_w, groups, cols, before):
        return update_call(for_m, for_w, groups, cols, before)

    new_momentum = update(for_m, (), [[r0, r1]], piece[:1], ())
    new_weight = update((), for_w, [[r0, r1]], piece[:1], ())
    out = *new_weight, *new_momentum
    out = update(for_m, for_w, [[a0, a1], [b0, b1]], near, out)
    out = update(for_m, for_w, [[e0, f0, e1, f1]], piece[3:], out)
    return (*out, new_factor)


def solution(mesh):
    rows, cols = mesh.shape["row"], mesh.shape["col"]
    local_rows, width = ROWS // rows, COLS // cols
    fits = (rows, cols, RANK) == (4, 8, 2 * HALF) and local_rows % 1024 == 0 and width % 512 == 0

    def per_device(*args):
        if not fits:
            return general(*args)
        return square(*args)

    return jax.shard_map(
        per_device,
        mesh=mesh,
        in_specs=(P("row", "col"), P("row", "col"), P("row", "col"), P(("col", "row"), None)),
        out_specs=(P("row", "col"), P("row", "col"), P(("col", "row"), None)),
        check_vma=False,
    )
```

```python
import functools

import jax
import jax.numpy as jnp
from jax import lax
from jax.experimental import pallas as pl
from jax.experimental.pallas import tpu as pltpu
from jax.sharding import PartitionSpec as P


ROWS = 4096
COLS = 28672
RANK = 512
F32 = jnp.float32
BF16 = jnp.bfloat16
HIGHEST = lax.Precision.HIGHEST
NB = 128
HALF = 256
VMEM = pl.BlockSpec(memory_space=pltpu.VMEM)
LIMIT = 40 * 2**20
WIDE = 52 * 2**20
WIDER = 56 * 2**20


def general(momentum, gradient, weight, right_factor):
    high = HIGHEST
    buffer = momentum + gradient.astype(F32)
    whole = lax.all_gather(right_factor, "row", axis=0, tiled=True)
    partial_proj = jnp.dot(buffer, whole, precision=high, preferred_element_type=F32)
    proj = lax.psum(partial_proj, "col")
    gram = lax.psum(jnp.dot(proj.T, proj, precision=high, preferred_element_type=F32), "row")
    chol = jnp.linalg.cholesky(gram)
    ortho = lax.linalg.triangular_solve(chol, proj, left_side=False, lower=True, transpose_a=True)
    share = lax.dot_general(
        buffer, ortho, (((0,), (0,)), ((), ())), precision=high, preferred_element_type=F32
    )
    right_share = lax.psum_scatter(share, "row", scatter_dimension=0, tiled=True)
    squares = lax.psum(jnp.sum(right_share * right_share, axis=0), ("row", "col"))
    scale = lax.rsqrt(squares + 1e-06)
    new_factor = right_share * scale
    right = lax.all_gather(right_share, "row", axis=0, tiled=True)
    new_momentum = buffer - 0.05 * jnp.dot(
        ortho, right.T, precision=high, preferred_element_type=F32
    )
    coef = 0.3 * (ROWS * COLS / RANK) ** 0.5
    update = jnp.dot(ortho, (right * scale).T, precision=high, preferred_element_type=F32)
    new_weight = (weight.astype(F32) - coef * update).astype(BF16)
    return (new_weight, new_momentum, new_factor)


def split(x):
    hi = x.astype(BF16)
    return hi, (x - hi.astype(F32)).astype(BF16)


def mul(a, b, ca=1, cb=0):
    return lax.dot_general(a, b, (((ca,), (cb,)), ((), ())), preferred_element_type=F32)


def exact(a, b, ca=1, cb=0):
    return lax.dot_general(
        a, b, (((ca,), (cb,)), ((), ())), precision=HIGHEST, preferred_element_type=F32
    )


def params(limit=LIMIT):
    return pltpu.CompilerParams(vmem_limit_bytes=limit)


def cost(flops, nbytes):
    return pl.CostEstimate(flops=int(flops), bytes_accessed=int(nbytes), transcendentals=0)


def mul3(a, b, ca=1, cb=0):
    (ah, al), (bh, bl) = a, b
    return mul(ah, bh, ca, cb) + mul(ah, bl, ca, cb) + mul(al, bh, ca, cb)


def whole_spec(shape):
    return pl.BlockSpec(shape, lambda *_: (0,) * len(shape))


def split_kernel(m_ref, g_ref, h_ref, l_ref):
    h_ref[...], l_ref[...] = split(m_ref[...] + g_ref[...].astype(F32))


def split_call(momentum, gradient):
    rows, width = momentum.shape
    spec = pl.BlockSpec((rows // 8, width), lambda i: (i, 0))
    out = jax.ShapeDtypeStruct(momentum.shape, BF16)
    return pl.pallas_call(
        split_kernel,
        grid=(8,),
        in_specs=[spec] * 2,
        out_specs=[spec] * 2,
        out_shape=[out] * 2,
        compiler_params=params(),
        name="split",
        cost_estimate=cost(4 * rows * width, 10 * rows * width),
    )(momentum, gradient)


def proj_kernel(sizes, first, col_ref, row_ref, z_ref, bh_ref, bl_ref, *refs):
    groups, accs = refs[: sum(sizes)], refs[sum(sizes) : -4]
    outs = refs[-4:-2]
    rh, rl = refs[-2:]
    k, i = pl.program_id(0), pl.program_id(1)

    @pl.when(i == 0)
    def _():
        for p, size in enumerate(sizes):
            mine = groups[sum(sizes[:p]) : sum(sizes[: p + 1])]

            @pl.when(k == p)
            def _(mine=mine):
                h = mine[0].shape[0]
                for q, ref in enumerate(mine):
                    at = slice(q * h, (q + 1) * h)
                    rh[at, :], rl[at, :] = split(ref[...])

    term = mul3((bh_ref[...], bl_ref[...]), (rh[...], rl[...]))
    h = term.shape[0] // 2
    for s in range(2):

        @pl.when(i == s)
        def _(s=s):
            for u in range(2):
                at = pl.ds(pl.multiple_of((u ^ z_ref[0]) * h, h), h)
                part = term[u * h : (u + 1) * h, :]

                @pl.when(k == 0)
                def _():
                    outs[s][at, :] = part if first else accs[s][at, :] + part

                @pl.when(k != 0)
                def _():
                    outs[s][at, :] += part


def proj_call(pair, groups, cols, rows, z0, acc):
    n = len(groups)
    pieces = [x for group in groups for x in group]
    tm = pair[0].shape[0] // 2
    kp, c = pair[0].shape[1] // 4, pieces[0].shape[1]
    accs = () if acc is None else tuple(acc)
    spec = pl.BlockSpec((tm, kp), lambda k, i, col, row, z: (row[i], col[k]))
    out = jax.ShapeDtypeStruct((tm, c), F32)
    return pl.pallas_call(
        functools.partial(proj_kernel, [len(g) for g in groups], acc is None),
        grid_spec=pltpu.PrefetchScalarGridSpec(
            num_scalar_prefetch=3,
            grid=(n, 2),
            in_specs=[spec] * 2 + [whole_spec(x.shape) for x in pieces] + [whole_spec((tm, c))] * len(accs),
            out_specs=[whole_spec((tm, c))] * 2,
            scratch_shapes=[pltpu.VMEM((kp, c), BF16)] * 2,
        ),
        out_shape=[out] * 2,
        compiler_params=params(),
        cost_estimate=cost(12 * n * kp * c * tm, 8 * n * kp * tm),
    )(cols, rows, z0, *pair, *pieces, *accs)


def prep_kernel(nt, row_ref, core_ref, *refs):
    h_ref, l_ref, g_ref = refs[-3:]
    own, others = refs[:nt], refs[nt:-3]
    tm = own[0].shape[0]
    turned = []
    for p in range(nt):
        x = own[p][...].T
        at = pl.ds(pl.multiple_of(row_ref[p] * tm, tm), tm)
        h_ref[:, at], l_ref[:, at] = split(x)
        turned.append(x)

    def gram(with_):
        total = exact(turned[0], with_[0][...])
        for p in range(1, nt):
            total = total + exact(turned[p], with_[p][...])
        g_ref[...] = total

    if others:
        pl.when(core_ref[0] == 0)(lambda: gram(others))
        pl.when(core_ref[0] == 1)(lambda: gram(own))
    else:
        gram(own)


def prep_call(own, others, rows, core):
    nt = len(own)
    tm, c = own[0].shape
    turned = jax.ShapeDtypeStruct((c, nt * tm), BF16)
    return pl.pallas_call(
        functools.partial(prep_kernel, nt),
        grid_spec=pltpu.PrefetchScalarGridSpec(
            num_scalar_prefetch=2,
            grid=(),
            in_specs=[VMEM] * (nt + len(others)),
            out_specs=[VMEM] * 3,
        ),
        out_shape=[turned, turned, jax.ShapeDtypeStruct((c, c), F32)],
        compiler_params=params(),
        cost_estimate=cost(12 * nt * tm * c * c, 3 * 2**20),
    )(rows, core, *own, *others)


def far_kernel(col_ref, ph_ref, pl_ref, bh_ref, bl_ref, a_ref, b_ref, o_ref):
    k = pl.program_id(0)
    term = mul3((ph_ref[...], pl_ref[...]), (bh_ref[...], bl_ref[...]))
    h = a_ref.shape[0]

    @pl.when(k == 0)
    def _():
        a_ref[...], b_ref[...] = term[:h, :], term[h:, :]

    @pl.when(k == 1)
    def _():
        o_ref[...] = term


def halves_kernel(col_ref, ph_ref, pl_ref, bh_ref, bl_ref, *refs):
    k = pl.program_id(0)
    term = mul3((ph_ref[...], pl_ref[...]), (bh_ref[...], bl_ref[...]))
    h = refs[0].shape[0]
    for s in range(2):

        @pl.when(k == s)
        def _(s=s):
            refs[2 * s][...], refs[2 * s + 1][...] = term[:h, :], term[h:, :]


def right_call(kernel, pair, turned, cols):
    rows, width = pair[0].shape
    c = turned[0].shape[0]
    kp = width // 4
    spec = pl.BlockSpec((rows, kp), lambda k, col: (0, col[k]))
    full, half = ((c, kp), (c // 2, kp))
    outs = [half] * 2 + [full] if kernel is far_kernel else [half] * 4
    return pl.pallas_call(
        kernel,
        grid_spec=pltpu.PrefetchScalarGridSpec(
            num_scalar_prefetch=1,
            grid=(2,),
            in_specs=[VMEM] * 2 + [spec] * 2,
            out_specs=[whole_spec(s) for s in outs],
        ),
        out_shape=[jax.ShapeDtypeStruct(s, F32) for s in outs],
        compiler_params=params(),
        cost_estimate=cost(12 * kp * c * rows, 8 * kp * rows),
    )(cols, *turned, *pair)


def eliminate(d):
    n = d.shape[0]
    gs = n // 8
    sub = lax.broadcasted_iota(jnp.int32, (8, n), 0)
    lane = lax.broadcasted_iota(jnp.int32, (8, n), 1)
    left = [d[8 * g : 8 * g + 8, :] for g in range(gs)]
    right = [jnp.where(lane == sub + 8 * g, 1.0, 0.0).astype(F32) for g in range(gs)]
    wide = lambda x: jnp.broadcast_to(x, (8, n))
    for g in range(gs):
        cols = [
            [wide(left[t][:, 8 * g + e : 8 * g + e + 1]) for e in range(8)] for t in range(g, gs)
        ]
        for e in range(8):
            inv = 1.0 / wide(cols[0][e][e : e + 1, :])
            row_l = wide(left[g][e : e + 1, :]) * inv
            row_r = wide(right[g][e : e + 1, :]) * inv
            ahead = [wide(cols[0][f][e : e + 1, :]) * inv for f in range(e + 1, 8)]
            for t in range(g, gs):
                c = cols[t - g][e]
                if t == g:
                    if e == 7:
                        continue
                    c = jnp.where(sub > e, c, 0.0)
                for f in range(e + 1, 8):
                    cols[t - g][f] = cols[t - g][f] - c * ahead[f - e - 1]
                left[t] = left[t] - c * row_l
                right[t] = right[t] - c * row_r
    out = []
    for g in range(gs):
        pivot = jnp.sum(jnp.where(lane == sub + 8 * g, left[g], 0.0), axis=1, keepdims=True)
        out.append(right[g] * lax.rsqrt(pivot))
    return jnp.concatenate(out, axis=0)


def chol_inverse(a_ref, o_ref):
    def body(k, carry):
        at = pl.ds(pl.multiple_of(k * NB, NB), NB)
        o_ref[at, at] = eliminate(a_ref[at, at])

        @pl.when(k == 0)
        def _():
            panel = exact(a_ref[NB:, :NB], o_ref[:NB, :NB], 1, 1)
            a_ref[NB:, NB:] = a_ref[NB:, NB:] - exact(panel, panel, 1, 1)
            a_ref[NB:, :NB] = panel

        return carry

    lax.fori_loop(0, 2, body, 0)
    o_ref[:NB, NB:] = jnp.zeros((NB, NB), F32)
    o_ref[NB:, :NB] = -exact(o_ref[NB:, NB:], exact(a_ref[NB:, :NB], o_ref[:NB, :NB]))


def chol_first(g_ref, o_ref, a_ref):
    a_ref[...] = g_ref[...]
    chol_inverse(a_ref, o_ref)


def chol_second(core_ref, mine_ref, other_ref, x_ref, h_ref, l_ref, a_ref, o_ref):
    n = x_ref.shape[0]
    first = core_ref[0] == 0
    below = jnp.where(first, mine_ref[...], other_ref[...])
    corner = jnp.where(first, other_ref[...], mine_ref[...])
    x = x_ref[...]
    panel = exact(below, x, 1, 1)
    a_ref[...] = corner - exact(panel, panel, 1, 1)
    chol_inverse(a_ref, o_ref)
    y = o_ref[...]
    h_ref[:n, n:] = jnp.zeros((n, n), BF16)
    l_ref[:n, n:] = jnp.zeros((n, n), BF16)
    h_ref[:n, :n], l_ref[:n, :n] = split(x)
    h_ref[n:, n:], l_ref[n:, n:] = split(y)
    h_ref[n:, :n], l_ref[n:, :n] = split(-exact(y, exact(panel, x)))


def chol_calls(block, mine, other, core):
    n = block.shape[0]
    shape = jax.ShapeDtypeStruct((n, n), F32)
    x = pl.pallas_call(
        chol_first,
        in_specs=[VMEM],
        out_specs=VMEM,
        out_shape=shape,
        scratch_shapes=[pltpu.VMEM((n, n), F32)],
        compiler_params=params(),
        name="chol_first",
        cost_estimate=cost(10**10, 2**20),
    )(block)
    out = jax.ShapeDtypeStruct((2 * n, 2 * n), BF16)
    return pl.pallas_call(
        chol_second,
        grid_spec=pltpu.PrefetchScalarGridSpec(
            num_scalar_prefetch=1,
            grid=(),
            in_specs=[VMEM] * 3,
            out_specs=[VMEM] * 2,
            scratch_shapes=[pltpu.VMEM((n, n), F32)] * 2,
        ),
        out_shape=[out] * 2,
        compiler_params=params(),
        name="chol_second",
        cost_estimate=cost(10**10, 2**20),
    )(core, mine, other, x), x


def ortho_kernel(nt, nc, row_ref, ih_ref, il_ref, *refs):
    o_ref, h_ref = refs[-2:]
    i = pl.program_id(0)
    for p in range(nt):

        @pl.when(i == p)
        def _(p=p):
            x = jnp.concatenate([refs[j * nt + p][...] for j in range(nc)], axis=1)
            o = mul3(split(x), (ih_ref[...], il_ref[...]), 1, 1)
            o_ref[...] = o
            h_ref[...] = (0.05 * o).astype(BF16)


def ortho_call(chunks, inv, rows):
    nt, nc = len(chunks[0]), len(chunks)
    tm, c = chunks[0][0].shape
    spec = pl.BlockSpec((tm, nc * c), lambda i, row: (row[i], 0))
    return pl.pallas_call(
        functools.partial(ortho_kernel, nt, nc),
        grid_spec=pltpu.PrefetchScalarGridSpec(
            num_scalar_prefetch=1,
            grid=(nt,),
            in_specs=[whole_spec(inv[0].shape)] * 2 + [whole_spec((tm, c))] * (nt * nc),
            out_specs=[spec] * 2,
        ),
        out_shape=[
            jax.ShapeDtypeStruct((nt * tm, nc * c), F32),
            jax.ShapeDtypeStruct((nt * tm, nc * c), BF16),
        ],
        compiler_params=params(),
        name="ortho",
        cost_estimate=cost(6 * nt * tm * (nc * c) ** 2, 5 * 2**20),
    )(rows, *inv, *[x for chunk in chunks for x in chunk])


def turn_kernel(x_ref, a_ref, b_ref, o_ref):
    w = jnp.concatenate([a_ref[...], b_ref[...]], axis=0)
    o_ref[...] = mul3(split(x_ref[...]), split(w))


def turn_call(x, halves):
    shape = (x.shape[0], halves[0].shape[1])
    return pl.pallas_call(
        turn_kernel,
        in_specs=[VMEM] * 3,
        out_specs=VMEM,
        out_shape=jax.ShapeDtypeStruct(shape, F32),
        compiler_params=params(),
        name="turn",
        cost_estimate=cost(6 * shape[0] ** 2 * shape[1], 2 * 2**20),
    )(x, *halves)


def share_kernel(ih_ref, il_ref, t_ref, *refs):
    t_out, r_ref, s_ref = refs[-3:]
    c = t_ref.shape[0]
    w = jnp.concatenate([r[...] for r in refs[:-3]], axis=0)
    t_out[...] = mul3((ih_ref[c:, :], il_ref[c:, :]), split(w))
    r_ref[:, :c] = t_ref[...].T
    r_ref[:, c:] = t_out[...].T
    r = r_ref[...]
    s_ref[...] = jnp.sum(r * r, axis=0, keepdims=True)


def share_call(first, halves, inv):
    c, kp = first.shape
    n = inv[0].shape[0]
    shapes = (c, kp), (kp, n), (1, n)
    return pl.pallas_call(
        share_kernel,
        in_specs=[VMEM] * (3 + len(halves)),
        out_specs=[VMEM] * 3,
        out_shape=[jax.ShapeDtypeStruct(s, F32) for s in shapes],
        compiler_params=params(),
        name="share",
        cost_estimate=cost(6 * kp * n * c, 5 * 2**20),
    )(*inv, first, *halves)


def scale_kernel(coef, s_ref, r_ref, o_ref, f_ref, h_ref, l_ref):
    scale = lax.rsqrt(s_ref[...] + 1e-06)
    f_ref[...] = r_ref[...] * scale
    h_ref[...], l_ref[...] = split(o_ref[...] * (coef * scale))


def scale_call(squares, share, ortho, coef):
    rows, n = ortho.shape
    out = jax.ShapeDtypeStruct((rows, n), BF16)
    parts = 4
    spec = pl.BlockSpec((rows // parts, n), lambda i: (i, 0))
    fspec = pl.BlockSpec((share.shape[0] // parts, n), lambda i: (i, 0))
    return pl.pallas_call(
        functools.partial(scale_kernel, coef),
        grid=(parts,),
        in_specs=[whole_spec((1, n)), fspec, spec],
        out_specs=[fspec, spec, spec],
        out_shape=[jax.ShapeDtypeStruct(share.shape, F32), out, out],
        compiler_params=params(),
        name="scale",
        cost_estimate=cost(4 * rows * n, 12 * rows * n),
    )(squares, share, ortho)


def update_kernel(groups, with_m, with_w, col_ref, *refs):
    refs = list(refs)
    take = lambda count: [refs.pop(0) for _ in range(count)]
    oh, m_ref, g_ref = take(3) if with_m else (None,) * 3
    sh, sl, w_ref = take(3) if with_w else (None,) * 3
    pieces = take(sum(groups))
    rl, rh = refs.pop(), refs.pop()
    m_out = refs.pop() if with_m else None
    w_out = refs.pop() if with_w else None
    k, i = pl.program_id(0), pl.program_id(1)

    @pl.when(i == 0)
    def _():
        at = 0
        for q, size in enumerate(groups):
            mine = pieces[at : at + size]
            at += size

            @pl.when(k == q)
            def _(mine=mine):
                row = 0
                for ref in mine:
                    rows = slice(row, row + ref.shape[0])
                    rh[rows, :], rl[rows, :] = split(ref[...])
                    row += ref.shape[0]

    tm = (m_ref if with_m else w_ref).shape[0]
    rows = pl.ds(pl.multiple_of(i * tm, tm), tm)
    if with_m:
        m_out[...] = m_ref[...] + g_ref[...].astype(F32) - mul(oh[rows, :], rh[...])
    if with_w:
        up = mul3((sh[rows, :], sl[rows, :]), (rh[...], rl[...]))
        w_out[...] = (w_ref[...].astype(F32) - up).astype(BF16)


def update_call(for_m, for_w, groups, cols, before):
    n = len(groups)
    like = for_m[1] if for_m else for_w[2]
    rows, width = like.shape
    kp = width // 4
    tm = rows // 4
    pieces = [x for group in groups for x in group]
    rank = sum(x.shape[0] for x in groups[0])
    spec = pl.BlockSpec((tm, kp), lambda k, i, col: (i, col[k]))
    in_specs = ([VMEM, spec, spec] if for_m else []) + ([VMEM, VMEM, spec] if for_w else [])
    in_specs += [VMEM] * len(pieces)
    outs = ([BF16] if for_w else []) + ([F32] if for_m else [])
    units = (1 if for_m else 0) + (3 if for_w else 0)
    return pl.pallas_call(
        functools.partial(update_kernel, [len(g) for g in groups], bool(for_m), bool(for_w)),
        grid_spec=pltpu.PrefetchScalarGridSpec(
            num_scalar_prefetch=1,
            grid=(n, 4),
            in_specs=in_specs + [pl.BlockSpec(memory_space=pl.ANY)] * len(before),
            out_specs=[spec] * len(outs),
            scratch_shapes=[pltpu.VMEM((rank, kp), BF16)] * 2,
        ),
        out_shape=[jax.ShapeDtypeStruct((rows, width), dtype) for dtype in outs],
        input_output_aliases={1 + len(in_specs) + e: e for e in range(len(before))},
        compiler_params=params(WIDE if units == 4 else WIDER),
        cost_estimate=cost(2 * units * n * kp * rows * rank, 3 * units * n * kp * rows),
    )(cols, *for_m, *for_w, *pieces, *before)


def square(momentum, gradient, weight, right_factor):
    def move(a, axis, size, flip):
        return lax.ppermute(a, axis, [(s, s ^ flip) for s in range(size)])

    to_x = lambda a: move(a, "row", 4, 1)
    to_y = lambda a: move(a, "row", 4, 2)
    to_core = lambda a: move(a, "col", 8, 1)
    to_z = lambda a, flip=2: move(a, "col", 8, flip)
    row, col = lax.axis_index("row"), lax.axis_index("col")
    one = lambda x: jnp.reshape(x, (1,)).astype(jnp.int32)
    core, z0 = col % 2, (col // 2) % 2
    tile = jnp.arange(4, dtype=jnp.int32) ^ (core * 2 + z0)
    sides = jnp.arange(2, dtype=jnp.int32) ^ core
    piece = jnp.arange(4, dtype=jnp.int32) ^ row
    far, near = jnp.array([3, 0], jnp.int32) ^ row, piece[1:3]
    core, z0 = one(core), one(z0)
    coef = 0.3 * (ROWS * COLS / RANK) ** 0.5

    def first_hop(own):
        return to_x(own), to_y(own)

    def second_hop(bx, by):
        h = bx.shape[0] // 2
        return to_x(by[:h]), to_y(bx[h:])

    def add_cols(keep, give):
        s = keep + to_core(give)
        h = s.shape[0] // 2
        t = s[:h] + to_z(s[h:])
        t = t + to_z(t, 4)
        ct = to_core(t)
        o = to_z(t)
        return t, o, ct, to_core(o)

    def project(groups, cols, acc):
        return proj_call(pair, groups, cols, sides, z0, acc)

    own0, own1 = right_factor[:, :HALF], right_factor[:, HALF:]
    x0, y0 = first_hop(own0)
    pair = split_call(momentum, gradient)
    acc0 = project([[own0]], piece[:1], None)
    own1, x0, y0 = lax.optimization_barrier((own1, x0, y0))
    e0, f0 = second_hop(x0, y0)
    acc0 = project([[x0], [y0]], near, acc0)
    x1, y1 = first_hop(own1)
    proj0 = add_cols(*project([[e0, f0]], piece[3:], acc0))
    acc1 = project([[own1]], piece[:1], None)
    e1, f1 = second_hop(x1, y1)
    acc1 = project([[x1], [y1]], near, acc1)
    proj1 = add_cols(*project([[e1, f1]], piece[3:], acc1))

    def right(kernel, turned, cols):
        return right_call(kernel, pair, turned, cols)

    def sum_rows(turned):
        da, db, own = right(far_kernel, turned, far)
        got_x, got_y = to_x(da), to_y(db)
        xa, xb, ya, yb = right(halves_kernel, turned, near)
        xa, yb = to_x(xa), to_y(yb)
        xb, ya = to_x(xb + got_y), to_y(ya + got_x)
        h = xa.shape[0]
        return own[:h] + xa + ya, own[h:] + xb + yb

    def sum4(a):
        ax, ay = to_x(a), to_y(a)
        return (a + ax) + (ay + move(a, "row", 4, 3))

    *turned0, block = prep_call(proj0, (), tile, core)
    block = block + to_x(block)
    block = block + to_y(block)
    w0 = sum_rows(turned0)
    *turned1, mine = prep_call(proj1, proj0, tile, core)
    mine = sum4(mine)
    inv, corner = chol_calls(block, mine, to_core(mine), core)
    w1 = sum_rows(turned1)
    r0 = turn_call(corner, w0)
    a0, b0 = first_hop(r0)
    e0 = to_x(b0)
    r1, share, squares = share_call(r0, [*w0, *w1], inv)
    squares = sum4(squares)
    squares = squares + to_core(squares)
    squares = (squares + to_z(squares)) + (to_z(squares, 4) + to_z(squares, 6))
    a1, b1 = first_hop(r1)
    f1 = to_y(a1)
    ortho, left = ortho_call([proj0, proj1], inv, tile)
    new_factor, *lefts = scale_call(squares, share, ortho, coef)
    for_m, for_w = (left, momentum, gradient), (*lefts, weight)

    def update(for_m, for_w, groups, cols, before):
        return update_call(for_m, for_w, groups, cols, before)

    new_momentum = update(for_m, (), [[r0, r1]], piece[:1], ())
    new_weight = update((), for_w, [[r0, r1]], piece[:1], ())
    out = *new_weight, *new_momentum
    out = update(for_m, for_w, [[a0, a1], [b0, b1]], near, out)
    out = update(for_m, for_w, [[e0, f1]], piece[3:], out)
    return (*out, new_factor)


def solution(mesh):
    rows, cols = mesh.shape["row"], mesh.shape["col"]
    local_rows, width = ROWS // rows, COLS // cols
    fits = (rows, cols, RANK) == (4, 8, 2 * HALF) and local_rows % 1024 == 0 and width % 512 == 0

    def per_device(*args):
        if not fits:
            return general(*args)
        return square(*args)

    return jax.shard_map(
        per_device,
        mesh=mesh,
        in_specs=(P("row", "col"), P("row", "col"), P("row", "col"), P(("col", "row"), None)),
        out_specs=(P("row", "col"), P("row", "col"), P(("col", "row"), None)),
        check_vma=False,
    )
```

```python
import functools

import jax
import jax.numpy as jnp
from jax import lax
from jax.experimental import pallas as pl
from jax.experimental.pallas import tpu as pltpu
from jax.sharding import PartitionSpec as P


ROWS = 4096
COLS = 28672
RANK = 512
F32 = jnp.float32
BF16 = jnp.bfloat16
HIGHEST = lax.Precision.HIGHEST
NB = 128
HALF = 256
VMEM = pl.BlockSpec(memory_space=pltpu.VMEM)
LIMIT = 40 * 2**20
WIDE = 36 * 2**20
WIDER = 36 * 2**20


def general(momentum, gradient, weight, right_factor):
    high = HIGHEST
    buffer = momentum + gradient.astype(F32)
    whole = lax.all_gather(right_factor, "row", axis=0, tiled=True)
    partial_proj = jnp.dot(buffer, whole, precision=high, preferred_element_type=F32)
    proj = lax.psum(partial_proj, "col")
    gram = lax.psum(jnp.dot(proj.T, proj, precision=high, preferred_element_type=F32), "row")
    chol = jnp.linalg.cholesky(gram)
    ortho = lax.linalg.triangular_solve(chol, proj, left_side=False, lower=True, transpose_a=True)
    share = lax.dot_general(
        buffer, ortho, (((0,), (0,)), ((), ())), precision=high, preferred_element_type=F32
    )
    right_share = lax.psum_scatter(share, "row", scatter_dimension=0, tiled=True)
    squares = lax.psum(jnp.sum(right_share * right_share, axis=0), ("row", "col"))
    scale = lax.rsqrt(squares + 1e-06)
    new_factor = right_share * scale
    right = lax.all_gather(right_share, "row", axis=0, tiled=True)
    new_momentum = buffer - 0.05 * jnp.dot(
        ortho, right.T, precision=high, preferred_element_type=F32
    )
    coef = 0.3 * (ROWS * COLS / RANK) ** 0.5
    update = jnp.dot(ortho, (right * scale).T, precision=high, preferred_element_type=F32)
    new_weight = (weight.astype(F32) - coef * update).astype(BF16)
    return (new_weight, new_momentum, new_factor)


def split(x):
    hi = x.astype(BF16)
    return hi, (x - hi.astype(F32)).astype(BF16)


def mul(a, b, ca=1, cb=0):
    return lax.dot_general(a, b, (((ca,), (cb,)), ((), ())), preferred_element_type=F32)


def exact(a, b, ca=1, cb=0):
    return lax.dot_general(
        a, b, (((ca,), (cb,)), ((), ())), precision=HIGHEST, preferred_element_type=F32
    )


def params(limit=LIMIT):
    return pltpu.CompilerParams(vmem_limit_bytes=limit)


def cost(flops, nbytes):
    return pl.CostEstimate(flops=int(flops), bytes_accessed=int(nbytes), transcendentals=0)


def mul3(a, b, ca=1, cb=0):
    (ah, al), (bh, bl) = a, b
    return mul(ah, bh, ca, cb) + mul(ah, bl, ca, cb) + mul(al, bh, ca, cb)


def whole_spec(shape):
    return pl.BlockSpec(shape, lambda *_: (0,) * len(shape))


def split_kernel(m_ref, g_ref, h_ref, l_ref):
    h_ref[...], l_ref[...] = split(m_ref[...] + g_ref[...].astype(F32))


def split_call(momentum, gradient):
    rows, width = momentum.shape
    spec = pl.BlockSpec((rows // 8, width), lambda i: (i, 0))
    out = jax.ShapeDtypeStruct(momentum.shape, BF16)
    return pl.pallas_call(
        split_kernel,
        grid=(8,),
        in_specs=[spec] * 2,
        out_specs=[spec] * 2,
        out_shape=[out] * 2,
        compiler_params=params(),
        name="split",
        cost_estimate=cost(4 * rows * width, 10 * rows * width),
    )(momentum, gradient)


def proj_kernel(sizes, first, col_ref, row_ref, z_ref, bh_ref, bl_ref, *refs):
    groups, accs = refs[: sum(sizes)], refs[sum(sizes) : -4]
    outs = refs[-4:-2]
    rh, rl = refs[-2:]
    k, i = pl.program_id(0), pl.program_id(1)

    @pl.when(i == 0)
    def _():
        for p, size in enumerate(sizes):
            mine = groups[sum(sizes[:p]) : sum(sizes[: p + 1])]

            @pl.when(k == p)
            def _(mine=mine):
                h = mine[0].shape[0]
                for q, ref in enumerate(mine):
                    at = slice(q * h, (q + 1) * h)
                    rh[at, :], rl[at, :] = split(ref[...])

    term = mul3((bh_ref[...], bl_ref[...]), (rh[...], rl[...]))
    h = term.shape[0] // 2
    for s in range(2):

        @pl.when(i == s)
        def _(s=s):
            for u in range(2):
                at = pl.ds(pl.multiple_of((u ^ z_ref[0]) * h, h), h)
                part = term[u * h : (u + 1) * h, :]

                @pl.when(k == 0)
                def _():
                    outs[s][at, :] = part if first else accs[s][at, :] + part

                @pl.when(k != 0)
                def _():
                    outs[s][at, :] += part


def proj_call(pair, groups, cols, rows, z0, acc):
    n = len(groups)
    pieces = [x for group in groups for x in group]
    tm = pair[0].shape[0] // 2
    kp, c = pair[0].shape[1] // 4, pieces[0].shape[1]
    accs = () if acc is None else tuple(acc)
    spec = pl.BlockSpec((tm, kp), lambda k, i, col, row, z: (row[i], col[k]))
    out = jax.ShapeDtypeStruct((tm, c), F32)
    return pl.pallas_call(
        functools.partial(proj_kernel, [len(g) for g in groups], acc is None),
        grid_spec=pltpu.PrefetchScalarGridSpec(
            num_scalar_prefetch=3,
            grid=(n, 2),
            in_specs=[spec] * 2 + [whole_spec(x.shape) for x in pieces] + [whole_spec((tm, c))] * len(accs),
            out_specs=[whole_spec((tm, c))] * 2,
            scratch_shapes=[pltpu.VMEM((kp, c), BF16)] * 2,
        ),
        out_shape=[out] * 2,
        compiler_params=params(),
        cost_estimate=cost(12 * n * kp * c * tm, 8 * n * kp * tm),
    )(cols, rows, z0, *pair, *pieces, *accs)


def prep_kernel(nt, row_ref, core_ref, *refs):
    h_ref, l_ref, g_ref = refs[-3:]
    own, others = refs[:nt], refs[nt:-3]
    tm = own[0].shape[0]
    turned = []
    for p in range(nt):
        x = own[p][...].T
        at = pl.ds(pl.multiple_of(row_ref[p] * tm, tm), tm)
        h_ref[:, at], l_ref[:, at] = split(x)
        turned.append(x)

    def gram(with_):
        total = exact(turned[0], with_[0][...])
        for p in range(1, nt):
            total = total + exact(turned[p], with_[p][...])
        g_ref[...] = total

    if others:
        pl.when(core_ref[0] == 0)(lambda: gram(others))
        pl.when(core_ref[0] == 1)(lambda: gram(own))
    else:
        gram(own)


def prep_call(own, others, rows, core):
    nt = len(own)
    tm, c = own[0].shape
    turned = jax.ShapeDtypeStruct((c, nt * tm), BF16)
    return pl.pallas_call(
        functools.partial(prep_kernel, nt),
        grid_spec=pltpu.PrefetchScalarGridSpec(
            num_scalar_prefetch=2,
            grid=(),
            in_specs=[VMEM] * (nt + len(others)),
            out_specs=[VMEM] * 3,
        ),
        out_shape=[turned, turned, jax.ShapeDtypeStruct((c, c), F32)],
        compiler_params=params(),
        cost_estimate=cost(12 * nt * tm * c * c, 3 * 2**20),
    )(rows, core, *own, *others)


def far_kernel(col_ref, ph_ref, pl_ref, bh_ref, bl_ref, a_ref, b_ref, o_ref):
    k = pl.program_id(0)
    term = mul3((ph_ref[...], pl_ref[...]), (bh_ref[...], bl_ref[...]))
    h = a_ref.shape[0]

    @pl.when(k == 0)
    def _():
        a_ref[...], b_ref[...] = term[:h, :], term[h:, :]

    @pl.when(k == 1)
    def _():
        o_ref[...] = term


def halves_kernel(col_ref, ph_ref, pl_ref, bh_ref, bl_ref, *refs):
    k = pl.program_id(0)
    term = mul3((ph_ref[...], pl_ref[...]), (bh_ref[...], bl_ref[...]))
    h = refs[0].shape[0]
    for s in range(2):

        @pl.when(k == s)
        def _(s=s):
            refs[2 * s][...], refs[2 * s + 1][...] = term[:h, :], term[h:, :]


def right_call(kernel, pair, turned, cols):
    rows, width = pair[0].shape
    c = turned[0].shape[0]
    kp = width // 4
    spec = pl.BlockSpec((rows, kp), lambda k, col: (0, col[k]))
    full, half = ((c, kp), (c // 2, kp))
    outs = [half] * 2 + [full] if kernel is far_kernel else [half] * 4
    return pl.pallas_call(
        kernel,
        grid_spec=pltpu.PrefetchScalarGridSpec(
            num_scalar_prefetch=1,
            grid=(2,),
            in_specs=[VMEM] * 2 + [spec] * 2,
            out_specs=[whole_spec(s) for s in outs],
        ),
        out_shape=[jax.ShapeDtypeStruct(s, F32) for s in outs],
        compiler_params=params(),
        cost_estimate=cost(12 * kp * c * rows, 8 * kp * rows),
    )(cols, *turned, *pair)


def eliminate(d):
    n = d.shape[0]
    gs = n // 8
    sub = lax.broadcasted_iota(jnp.int32, (8, n), 0)
    lane = lax.broadcasted_iota(jnp.int32, (8, n), 1)
    left = [d[8 * g : 8 * g + 8, :] for g in range(gs)]
    right = [jnp.where(lane == sub + 8 * g, 1.0, 0.0).astype(F32) for g in range(gs)]
    wide = lambda x: jnp.broadcast_to(x, (8, n))
    for g in range(gs):
        cols = [
            [wide(left[t][:, 8 * g + e : 8 * g + e + 1]) for e in range(8)] for t in range(g, gs)
        ]
        for e in range(8):
            inv = 1.0 / wide(cols[0][e][e : e + 1, :])
            row_l = wide(left[g][e : e + 1, :]) * inv
            row_r = wide(right[g][e : e + 1, :]) * inv
            ahead = [wide(cols[0][f][e : e + 1, :]) * inv for f in range(e + 1, 8)]
            for t in range(g, gs):
                c = cols[t - g][e]
                if t == g:
                    if e == 7:
                        continue
                    c = jnp.where(sub > e, c, 0.0)
                for f in range(e + 1, 8):
                    cols[t - g][f] = cols[t - g][f] - c * ahead[f - e - 1]
                left[t] = left[t] - c * row_l
                right[t] = right[t] - c * row_r
    out = []
    for g in range(gs):
        pivot = jnp.sum(jnp.where(lane == sub + 8 * g, left[g], 0.0), axis=1, keepdims=True)
        out.append(right[g] * lax.rsqrt(pivot))
    return jnp.concatenate(out, axis=0)


def chol_inverse(a_ref, o_ref):
    def body(k, carry):
        at = pl.ds(pl.multiple_of(k * NB, NB), NB)
        o_ref[at, at] = eliminate(a_ref[at, at])

        @pl.when(k == 0)
        def _():
            panel = exact(a_ref[NB:, :NB], o_ref[:NB, :NB], 1, 1)
            a_ref[NB:, NB:] = a_ref[NB:, NB:] - exact(panel, panel, 1, 1)
            a_ref[NB:, :NB] = panel

        return carry

    lax.fori_loop(0, 2, body, 0)
    o_ref[:NB, NB:] = jnp.zeros((NB, NB), F32)
    o_ref[NB:, :NB] = -exact(o_ref[NB:, NB:], exact(a_ref[NB:, :NB], o_ref[:NB, :NB]))


def chol_first(g_ref, o_ref, a_ref):
    a_ref[...] = g_ref[...]
    chol_inverse(a_ref, o_ref)


def chol_second(core_ref, mine_ref, other_ref, x_ref, h_ref, l_ref, a_ref, o_ref):
    n = x_ref.shape[0]
    first = core_ref[0] == 0
    below = jnp.where(first, mine_ref[...], other_ref[...])
    corner = jnp.where(first, other_ref[...], mine_ref[...])
    x = x_ref[...]
    panel = exact(below, x, 1, 1)
    a_ref[...] = corner - exact(panel, panel, 1, 1)
    chol_inverse(a_ref, o_ref)
    y = o_ref[...]
    h_ref[:n, n:] = jnp.zeros((n, n), BF16)
    l_ref[:n, n:] = jnp.zeros((n, n), BF16)
    h_ref[:n, :n], l_ref[:n, :n] = split(x)
    h_ref[n:, n:], l_ref[n:, n:] = split(y)
    h_ref[n:, :n], l_ref[n:, :n] = split(-exact(y, exact(panel, x)))


def chol_calls(block, mine, other, core):
    n = block.shape[0]
    shape = jax.ShapeDtypeStruct((n, n), F32)
    x = pl.pallas_call(
        chol_first,
        in_specs=[VMEM],
        out_specs=VMEM,
        out_shape=shape,
        scratch_shapes=[pltpu.VMEM((n, n), F32)],
        compiler_params=params(),
        name="chol_first",
        cost_estimate=cost(10**10, 2**20),
    )(block)
    out = jax.ShapeDtypeStruct((2 * n, 2 * n), BF16)
    return pl.pallas_call(
        chol_second,
        grid_spec=pltpu.PrefetchScalarGridSpec(
            num_scalar_prefetch=1,
            grid=(),
            in_specs=[VMEM] * 3,
            out_specs=[VMEM] * 2,
            scratch_shapes=[pltpu.VMEM((n, n), F32)] * 2,
        ),
        out_shape=[out] * 2,
        compiler_params=params(),
        name="chol_second",
        cost_estimate=cost(10**10, 2**20),
    )(core, mine, other, x), x


def ortho_kernel(nt, nc, row_ref, ih_ref, il_ref, *refs):
    o_ref, h_ref = refs[-2:]
    i = pl.program_id(0)
    for p in range(nt):

        @pl.when(i == p)
        def _(p=p):
            x = jnp.concatenate([refs[j * nt + p][...] for j in range(nc)], axis=1)
            o = mul3(split(x), (ih_ref[...], il_ref[...]), 1, 1)
            at = pl.ds(pl.multiple_of(row_ref[p] * x.shape[0], x.shape[0]), x.shape[0])
            o_ref[at, :] = o
            h_ref[at, :] = (0.05 * o).astype(BF16)


def ortho_call(chunks, inv, rows):
    nt, nc = len(chunks[0]), len(chunks)
    tm, c = chunks[0][0].shape
    return pl.pallas_call(
        functools.partial(ortho_kernel, nt, nc),
        grid_spec=pltpu.PrefetchScalarGridSpec(
            num_scalar_prefetch=1,
            grid=(nt,),
            in_specs=[whole_spec(inv[0].shape)] * 2 + [whole_spec((tm, c))] * (nt * nc),
            out_specs=[VMEM] * 2,
        ),
        out_shape=[
            jax.ShapeDtypeStruct((nt * tm, nc * c), F32),
            jax.ShapeDtypeStruct((nt * tm, nc * c), BF16),
        ],
        compiler_params=params(),
        name="ortho",
        cost_estimate=cost(6 * nt * tm * (nc * c) ** 2, 5 * 2**20),
    )(rows, *inv, *[x for chunk in chunks for x in chunk])


def turn_kernel(x_ref, a_ref, b_ref, o_ref):
    w = jnp.concatenate([a_ref[...], b_ref[...]], axis=0)
    o_ref[...] = mul3(split(x_ref[...]), split(w))


def turn_call(x, halves):
    shape = (x.shape[0], halves[0].shape[1])
    return pl.pallas_call(
        turn_kernel,
        in_specs=[VMEM] * 3,
        out_specs=VMEM,
        out_shape=jax.ShapeDtypeStruct(shape, F32),
        compiler_params=params(),
        name="turn",
        cost_estimate=cost(6 * shape[0] ** 2 * shape[1], 2 * 2**20),
    )(x, *halves)


def share_kernel(ih_ref, il_ref, t_ref, *refs):
    t_out, r_ref, s_ref = refs[-3:]
    c = t_ref.shape[0]
    w = jnp.concatenate([r[...] for r in refs[:-3]], axis=0)
    t_out[...] = mul3((ih_ref[c:, :], il_ref[c:, :]), split(w))
    r_ref[:, :c] = t_ref[...].T
    r_ref[:, c:] = t_out[...].T
    r = r_ref[...]
    s_ref[...] = jnp.sum(r * r, axis=0, keepdims=True)


def share_call(first, halves, inv):
    c, kp = first.shape
    n = inv[0].shape[0]
    shapes = (c, kp), (kp, n), (1, n)
    return pl.pallas_call(
        share_kernel,
        in_specs=[VMEM] * (3 + len(halves)),
        out_specs=[VMEM] * 3,
        out_shape=[jax.ShapeDtypeStruct(s, F32) for s in shapes],
        compiler_params=params(),
        name="share",
        cost_estimate=cost(6 * kp * n * c, 5 * 2**20),
    )(*inv, first, *halves)


def scale_kernel(coef, s_ref, r_ref, o_ref, f_ref, h_ref, l_ref):
    scale = lax.rsqrt(s_ref[...] + 1e-06)
    f_ref[...] = r_ref[...] * scale
    rows = o_ref.shape[0]
    at = pl.ds(pl.multiple_of(pl.program_id(0) * rows, rows), rows)
    h_ref[at, :], l_ref[at, :] = split(o_ref[...] * (coef * scale))


def scale_call(squares, share, ortho, coef):
    rows, n = ortho.shape
    out = jax.ShapeDtypeStruct((rows, n), BF16)
    parts = 4
    spec = pl.BlockSpec((rows // parts, n), lambda i: (i, 0))
    fspec = pl.BlockSpec((share.shape[0] // parts, n), lambda i: (i, 0))
    return pl.pallas_call(
        functools.partial(scale_kernel, coef),
        grid=(parts,),
        in_specs=[whole_spec((1, n)), fspec, spec],
        out_specs=[fspec, VMEM, VMEM],
        out_shape=[jax.ShapeDtypeStruct(share.shape, F32), out, out],
        compiler_params=params(),
        name="scale",
        cost_estimate=cost(4 * rows * n, 12 * rows * n),
    )(squares, share, ortho)


def update_kernel(groups, with_m, with_w, col_ref, *refs):
    refs = list(refs)
    take = lambda count: [refs.pop(0) for _ in range(count)]
    oh, m_ref, g_ref = take(3) if with_m else (None,) * 3
    sh, sl, w_ref = take(3) if with_w else (None,) * 3
    pieces = take(sum(groups))
    rl, rh = refs.pop(), refs.pop()
    m_out = refs.pop() if with_m else None
    w_out = refs.pop() if with_w else None
    k, i = pl.program_id(0), pl.program_id(1)

    @pl.when(i == 0)
    def _():
        at = 0
        for q, size in enumerate(groups):
            mine = pieces[at : at + size]
            at += size

            @pl.when(k == q)
            def _(mine=mine):
                row = 0
                for ref in mine:
                    rows = slice(row, row + ref.shape[0])
                    rh[rows, :], rl[rows, :] = split(ref[...])
                    row += ref.shape[0]

    tm = (m_ref if with_m else w_ref).shape[0]
    rows = pl.ds(pl.multiple_of(i * tm, tm), tm)
    if with_m:
        m_out[...] = m_ref[...] + g_ref[...].astype(F32) - mul(oh[rows, :], rh[...])
    if with_w:
        up = mul3((sh[rows, :], sl[rows, :]), (rh[...], rl[...]))
        w_out[...] = (w_ref[...].astype(F32) - up).astype(BF16)


def update_call(for_m, for_w, groups, cols, before):
    n = len(groups)
    like = for_m[1] if for_m else for_w[2]
    rows, width = like.shape
    kp = width // 4
    tm = rows // 4
    pieces = [x for group in groups for x in group]
    rank = sum(x.shape[0] for x in groups[0])
    spec = pl.BlockSpec((tm, kp), lambda k, i, col: (i, col[k]))
    in_specs = ([VMEM, spec, spec] if for_m else []) + ([VMEM, VMEM, spec] if for_w else [])
    in_specs += [VMEM] * len(pieces)
    outs = ([BF16] if for_w else []) + ([F32] if for_m else [])
    units = (1 if for_m else 0) + (3 if for_w else 0)
    return pl.pallas_call(
        functools.partial(update_kernel, [len(g) for g in groups], bool(for_m), bool(for_w)),
        grid_spec=pltpu.PrefetchScalarGridSpec(
            num_scalar_prefetch=1,
            grid=(n, 4),
            in_specs=in_specs + [pl.BlockSpec(memory_space=pl.ANY)] * len(before),
            out_specs=[spec] * len(outs),
            scratch_shapes=[pltpu.VMEM((rank, kp), BF16)] * 2,
        ),
        out_shape=[jax.ShapeDtypeStruct((rows, width), dtype) for dtype in outs],
        input_output_aliases={1 + len(in_specs) + e: e for e in range(len(before))},
        compiler_params=params(WIDE if units == 4 else WIDER),
        cost_estimate=cost(2 * units * n * kp * rows * rank, 3 * units * n * kp * rows),
    )(cols, *for_m, *for_w, *pieces, *before)


def square(momentum, gradient, weight, right_factor):
    def move(a, axis, size, flip):
        return lax.ppermute(a, axis, [(s, s ^ flip) for s in range(size)])

    to_x = lambda a: move(a, "row", 4, 1)
    to_y = lambda a: move(a, "row", 4, 2)
    to_core = lambda a: move(a, "col", 8, 1)
    to_z = lambda a, flip=2: move(a, "col", 8, flip)
    row, col = lax.axis_index("row"), lax.axis_index("col")
    one = lambda x: jnp.reshape(x, (1,)).astype(jnp.int32)
    core, z0 = col % 2, (col // 2) % 2
    tile = jnp.arange(4, dtype=jnp.int32) ^ (core * 2 + z0)
    sides = jnp.arange(2, dtype=jnp.int32) ^ core
    piece = jnp.arange(4, dtype=jnp.int32) ^ row
    far, near = jnp.array([3, 0], jnp.int32) ^ row, piece[1:3]
    core, z0 = one(core), one(z0)
    coef = 0.3 * (ROWS * COLS / RANK) ** 0.5

    def first_hop(own):
        return to_x(own), to_y(own)

    def second_hop(bx, by):
        h = bx.shape[0] // 2
        return to_x(by[:h]), to_y(bx[h:])

    def add_cols(keep, give):
        s = keep + to_core(give)
        h = s.shape[0] // 2
        t = s[:h] + to_z(s[h:])
        t = t + to_z(t, 4)
        ct = to_core(t)
        o = to_z(t)
        return t, o, ct, to_core(o)

    def project(groups, cols, acc):
        return proj_call(pair, groups, cols, sides, z0, acc)

    own0, own1 = right_factor[:, :HALF], right_factor[:, HALF:]
    x0, y0 = first_hop(own0)
    pair = split_call(momentum, gradient)
    acc0 = project([[own0]], piece[:1], None)
    own1, x0, y0 = lax.optimization_barrier((own1, x0, y0))
    e0, f0 = second_hop(x0, y0)
    acc0 = project([[x0], [y0]], near, acc0)
    x1, y1 = first_hop(own1)
    proj0 = add_cols(*project([[e0, f0]], piece[3:], acc0))
    acc1 = project([[own1]], piece[:1], None)
    e1, f1 = second_hop(x1, y1)
    acc1 = project([[x1], [y1]], near, acc1)
    proj1 = add_cols(*project([[e1, f1]], piece[3:], acc1))

    def right(kernel, turned, cols):
        return right_call(kernel, pair, turned, cols)

    def sum_rows(turned):
        da, db, own = right(far_kernel, turned, far)
        got_x, got_y = to_x(da), to_y(db)
        xa, xb, ya, yb = right(halves_kernel, turned, near)
        xa, yb = to_x(xa), to_y(yb)
        xb, ya = to_x(xb + got_y), to_y(ya + got_x)
        h = xa.shape[0]
        return own[:h] + xa + ya, own[h:] + xb + yb

    def sum4(a):
        ax, ay = to_x(a), to_y(a)
        return (a + ax) + (ay + move(a, "row", 4, 3))

    *turned0, block = prep_call(proj0, (), tile, core)
    block = sum4(block)
    w0 = sum_rows(turned0)
    *turned1, mine = prep_call(proj1, proj0, tile, core)
    mine = sum4(mine)
    inv, corner = chol_calls(block, mine, to_core(mine), core)
    w1 = sum_rows(turned1)
    r0 = turn_call(corner, w0)
    a0, b0 = first_hop(r0)
    e0 = to_x(b0)
    r1, share, squares = share_call(r0, [*w0, *w1], inv)
    squares = sum4(squares)
    squares = squares + to_core(squares)
    squares = (squares + to_z(squares)) + (to_z(squares, 4) + to_z(squares, 6))
    a1, b1 = first_hop(r1)
    f1 = to_y(a1)
    ortho, left = ortho_call([proj0, proj1], inv, tile)
    new_factor, *lefts = scale_call(squares, share, ortho, coef)
    for_m, for_w = (left, momentum, gradient), (*lefts, weight)

    def update(for_m, for_w, groups, cols, before):
        return update_call(for_m, for_w, groups, cols, before)

    new_momentum = update(for_m, (), [[r0, r1]], piece[:1], ())
    new_weight = update((), for_w, [[r0, r1]], piece[:1], ())
    out = *new_weight, *new_momentum
    out = update(for_m, for_w, [[a0, a1], [b0, b1]], near, out)
    out = update(for_m, for_w, [[e0, f1]], piece[3:], out)
    return (*out, new_factor)


def solution(mesh):
    rows, cols = mesh.shape["row"], mesh.shape["col"]
    local_rows, width = ROWS // rows, COLS // cols
    fits = (rows, cols, RANK) == (4, 8, 2 * HALF) and local_rows % 1024 == 0 and width % 512 == 0

    def per_device(*args):
        if not fits:
            return general(*args)
        return square(*args)

    return jax.shard_map(
        per_device,
        mesh=mesh,
        in_specs=(P("row", "col"), P("row", "col"), P("row", "col"), P(("col", "row"), None)),
        out_specs=(P("row", "col"), P("row", "col"), P(("col", "row"), None)),
        check_vma=False,
    )
```
